32 devices in a mesh: row: 4 (over x, core), col: 2 (over y), chan: 4 (over z).
Axes of the slice: x: 2, y: 2, z: 4, core: 2. Of those that a mesh axis runs over, the one named last changes fastest.
Arguments:
- features: bfloat16 [2048, 72, 36], P('chan', 'row', 'col'), may hold values from -6 to 6
- dilated_weight: bfloat16 [3, 3, 3, 2048, 256], P(None, None, None, 'chan'), may hold values from -0.0625 to 0.0625
- point_weight: bfloat16 [2048, 256], P('chan'), may hold values from -0.1875 to 0.1875
- branch_gain: float32 [256, 4], P('chan'), may hold values from 0.5 to 2
- branch_shift: float32 [256, 4], P('chan'), may hold values from -3 to 3
- project_weight: bfloat16 [256, 4, 256], P('chan'), may hold values from -0.25 to 0.25
- project_shift: float32 [256], P('chan'), may hold values from -3 to 3
- cotangent: bfloat16 [256, 72, 36], P('chan', 'row', 'col'), may hold values from -6 to 6
Outputs:
- mixed_out: bfloat16 [256, 72, 36], P('chan', 'row', 'col')
- input_grad: bfloat16 [2048, 72, 36], P('chan', 'row', 'col')
- dilated_grad: bfloat16 [3, 3, 3, 2048, 256], P(None, None, None, 'chan')
- point_grad: bfloat16 [2048, 256], P('chan')
- project_grad: bfloat16 [256, 4, 256], P('chan')
The draws below stay inside these ranges and needn't reach their ends.
All inputs are finite; a program needn't handle non-finite values.
Results may differ from the reference program's by a relative error of at most 0.007.
Values may be sent and summed in bfloat16 or wider, within the bound.
A program may use at most 128 MiB of HBM per device.

```python
import math
import jax
import jax.numpy as jnp

CIN = 2048
BR = 256
RATE_STEP = 6
MAP_H = 72
MAP_W = 36


def spiked(values, key, source, target, shards_of, factor):
    owner, partner = [(jnp.arange(values.shape[dim]) // (values.shape[dim] // shards_of)).reshape([-1 if axis == dim else 1 for axis in range(values.ndim)]) for dim in (source, target)]
    chosen = jax.random.permutation(key, shards_of)[partner]
    strong = (owner == chosen) | (owner == (partner + shards_of // 2) % shards_of)
    return jnp.where(strong, factor * values, values)


def block_scale(own_key, extent, split, smallest, high):
    factor_of, own = 1.0, jax.random.fold_in(own_key, 6)
    for position, parts in split:
        heights = jnp.exp(jax.random.uniform(jax.random.fold_in(own, position), (parts,), jnp.float32, smallest / len(split), high / len(split)))
        factor_of = factor_of * jnp.repeat(heights, extent[position] // parts).reshape([-1 if axis == position else 1 for axis in range(len(extent))])
    return factor_of


def gaussian(stream_key, dims, scale, bound, cuts=(), dtype=jnp.bfloat16):
    drawn = jax.random.normal(stream_key, dims, jnp.float32) * scale
    if len(cuts) > 0:
        drawn = block_scale(stream_key, dims, cuts, -0.22, 0.18) * drawn
    return jnp.clip(drawn, min=-bound, max=bound).astype(dtype)


def bell_draw_with(stream_key, dims, deviation, reach, split, heavy, held_as=jnp.bfloat16):
    entries = deviation * jax.random.normal(stream_key, dims, jnp.float32)
    if split:
        entries = entries * block_scale(stream_key, dims, split, -0.22, 0.18)
    return jnp.clip(spiked(entries, jax.random.fold_in(stream_key, 3), *heavy), -reach, reach).astype(held_as)


def setup_inputs(seed: int = 0) -> dict:
    splits = jax.random.split(jax.random.key(seed), 9)
    features = gaussian(splits[0], (CIN, MAP_H, MAP_W), 1.0, 6.0, ((0, 4), (1, 4), (2, 2)))
    dilated_weight = bell_draw_with(splits[1], (3, 3, 3, CIN, BR), (9 * CIN) ** -0.5, 0.0625, ((3, 4),), (3, 4, 4, 2.0))
    point_weight = bell_draw_with(splits[2], (CIN, BR), CIN ** -0.5, 0.1875, ((0, 4),), (0, 1, 4, 2.0))
    branch_gain = jnp.clip(jnp.exp(math.log(2.0) - 1.3862944 * jax.random.uniform(splits[3], (BR, 4), jnp.float32) ** block_scale(splits[3], (BR, 4), ((0, 4),), -0.2, 0.2)), 0.5, 2.0)
    branch_shift = gaussian(splits[4], (BR, 4), 0.5, 3.0, ((0, 4),), jnp.float32)
    project_weight = bell_draw_with(splits[5], (BR, 4, BR), (4 * BR) ** -0.5, 0.25, ((0, 4),), (0, 2, 4, 2.0))
    project_shift = gaussian(splits[6], (BR,), 0.5, 3.0, ((0, 4),), jnp.float32)
    cotangent = gaussian(splits[7], (BR, MAP_H, MAP_W), 1.0, 6.0, ((0, 4), (1, 4), (2, 2)))
    return {"features": features, "dilated_weight": dilated_weight, "point_weight": point_weight, "branch_gain": branch_gain, "branch_shift": branch_shift, "project_weight": project_weight, "project_shift": project_shift, "cotangent": cotangent}


def silu_slope(values):
    logistic = jax.nn.sigmoid(values)
    return logistic * (1.0 + values * (1.0 - logistic))


def reference(features, dilated_weight, point_weight, branch_gain, branch_shift, project_weight, project_shift, cotangent):
    margin = 3 * RATE_STEP
    pixels = MAP_H * MAP_W
    feats = features.astype(jnp.float32)
    padded = jnp.pad(feats, ((0, 0), (margin, margin), (margin, margin)))

    def window(array, top, left):
        return array[:, top:top + MAP_H, left:left + MAP_W].reshape(array.shape[0], pixels)

    center = window(padded, margin, margin)
    point_f = point_weight.astype(jnp.float32)
    dilated_f = dilated_weight.astype(jnp.float32)
    branch_list = [jnp.dot(point_f.T, center, preferred_element_type=jnp.float32)]
    for branch in range(3):
        dilation = (branch + 1) * RATE_STEP
        total = jnp.zeros((BR, pixels), jnp.float32)
        for row_tap in range(3):
            for col_tap in range(3):
                shifted = window(padded, margin + (row_tap - 1) * dilation, margin + (col_tap - 1) * dilation)
                total = total + jnp.dot(dilated_f[branch, row_tap, col_tap].T, shifted, preferred_element_type=jnp.float32)
        branch_list.append(total)
    branch_pre = jnp.stack(branch_list, axis=1)
    branch_act = branch_pre * branch_gain[:, :, None] + branch_shift[:, :, None]
    hidden = jax.nn.silu(branch_act).astype(jnp.bfloat16)
    hidden_f = hidden.astype(jnp.float32)
    project_f = project_weight.astype(jnp.float32)
    mixed = jnp.einsum("obq,obp->qp", project_f, hidden_f)
    mixed_act = mixed + project_shift[:, None]
    mixed_out = jax.nn.silu(mixed_act).astype(jnp.bfloat16).reshape(BR, MAP_H, MAP_W)
    mixed_grad = (cotangent.reshape(BR, pixels).astype(jnp.float32) * silu_slope(mixed_act)).astype(jnp.bfloat16)
    mixed_grad_f = mixed_grad.astype(jnp.float32)
    hidden_grad = jnp.einsum("obq,qp->obp", project_f, mixed_grad_f)
    project_grad = jnp.einsum("obp,qp->obq", hidden_f, mixed_grad_f).astype(jnp.bfloat16)
    branch_grad = (hidden_grad * silu_slope(branch_act) * branch_gain[:, :, None]).astype(jnp.bfloat16)
    grad_f = branch_grad.astype(jnp.float32)
    point_grad = jnp.dot(center, grad_f[:, 0].T, preferred_element_type=jnp.float32).astype(jnp.bfloat16)
    input_total = jnp.dot(point_f, grad_f[:, 0], preferred_element_type=jnp.float32)
    dilated_list = []
    for branch in range(3):
        dilation = (branch + 1) * RATE_STEP
        grad_pad = jnp.pad(grad_f[:, branch + 1].reshape(BR, MAP_H, MAP_W), ((0, 0), (margin, margin), (margin, margin)))
        for row_tap in range(3):
            for col_tap in range(3):
                shifted = window(padded, margin + (row_tap - 1) * dilation, margin + (col_tap - 1) * dilation)
                dilated_list.append(jnp.dot(shifted, grad_f[:, branch + 1].T, preferred_element_type=jnp.float32))
                back = window(grad_pad, margin - (row_tap - 1) * dilation, margin - (col_tap - 1) * dilation)
                input_total = input_total + jnp.dot(dilated_f[branch, row_tap, col_tap], back, preferred_element_type=jnp.float32)
    dilated_grad = jnp.stack(dilated_list).reshape(3, 3, 3, CIN, BR).astype(jnp.bfloat16)
    input_grad = input_total.astype(jnp.bfloat16).reshape(CIN, MAP_H, MAP_W)
    return (mixed_out, input_grad, dilated_grad, point_grad, project_grad)
```

```python
import functools

import jax
import jax.numpy as jnp
from jax import lax
from jax.experimental import pallas as pl
from jax.experimental.pallas import tpu as pltpu
from jax.sharding import PartitionSpec as P

RATE_STEP = 6
SLOT = 8
MARGIN_RUNS = 3
MARGIN_ROWS = 3 * RATE_STEP * SLOT
MESH = pl.DeviceIdType.MESH
VMEM = pltpu.VMEM
LIMIT = 67_000_000


def sigmoid(v):
    return 1.0 / (1.0 + jnp.exp(-v))


def silu_slope(values):
    logistic = jax.nn.sigmoid(values)
    return logistic * (1.0 + values * (1.0 - logistic))


def to_runs(cells):
    count, tile_h, tile_w = cells.shape
    runs = tile_w // RATE_STEP
    cells = cells.reshape(count, tile_h, runs, RATE_STEP)
    cells = jnp.pad(cells, ((0, 0), (0, 0), (0, 0), (0, SLOT - RATE_STEP)))
    return cells.transpose(2, 1, 3, 0).reshape(runs, tile_h * SLOT, count)


def from_runs(cells, tile_h, tile_w):
    runs = tile_w // RATE_STEP
    count = cells.shape[-1]
    cells = cells.reshape(runs, tile_h, SLOT, count)[:, :, :RATE_STEP]
    return cells.transpose(3, 1, 0, 2).reshape(count, tile_h, tile_w)


def spread_kernel(n_row, n_col, x_ref, out_ref, local_sem, send_sems, recv_sems):
    n_hi = n_row // 2
    row = lax.axis_index("row")
    col = lax.axis_index("col")
    hi, core = row // 2, row % 2
    runs, rows, _ = x_ref.shape
    first = (rows // 2 + 15) // 16 * 16
    starts, sizes = (0, first), (first, rows - first)

    hi_peer = [lax.rem(hi + d, n_hi) for d in range(n_hi)]
    hi_from = [lax.rem(hi - d + n_hi, n_hi) for d in range(n_hi)]
    col_peer = [lax.rem(col + d, n_col) for d in range(n_col)]
    col_from = [lax.rem(col - d + n_col, n_col) for d in range(n_col)]
    sibling = {"row": hi * 2 + 1 - core}
    partners = [sibling]
    partners += [{"row": hi_peer[d] * 2 + core} for d in range(1, n_hi)]
    partners += [{"col": col_peer[d]} for d in range(1, n_col)]

    barrier = pltpu.get_barrier_semaphore()
    for who in partners:
        pl.semaphore_signal(barrier, inc=1, device_id=who, device_id_type=MESH)

    dtype = out_ref.dtype
    total_runs, total_rows, width = out_ref.shape
    edge = jnp.zeros((MARGIN_ROWS, width), dtype)

    def clear_run(u, _):
        for at in (u, total_runs - MARGIN_RUNS + u):
            for y in range(0, total_rows, MARGIN_ROWS):
                out_ref[at, pl.ds(y, MARGIN_ROWS), :] = edge
        return 0

    def clear_ends(u, _):
        out_ref[u, pl.ds(0, MARGIN_ROWS), :] = edge
        out_ref[u, pl.ds(total_rows - MARGIN_ROWS, MARGIN_ROWS), :] = edge
        return 0

    pl.semaphore_wait(barrier, len(partners))

    def place(h, hi_, core_, col_):
        return out_ref.at[
            pl.ds(MARGIN_RUNS + runs * col_, runs),
            pl.ds(pl.multiple_of(MARGIN_ROWS + (hi_ * 2 + core_) * rows + starts[h], 16), sizes[h]),
            :,
        ]

    sent = []

    def send(h, dh, dc, who, slot):
        if dh == 0 and dc == 0:
            src = x_ref.at[:, pl.ds(starts[h], sizes[h]), :]
        else:
            src = place(h, hi_from[dh], core, col_from[dc])
        copy = pltpu.make_async_remote_copy(
            src_ref=src,
            dst_ref=place(h, hi_from[dh], core, col_from[dc]),
            send_sem=send_sems.at[len(sent)],
            recv_sem=recv_sems.at[slot],
            device_id=who,
            device_id_type=MESH,
        )
        copy.start()
        sent.append(copy)

    def slot_of(h, dh, dc, side):
        return ((h * n_hi + dh) * n_col + dc) * 2 + side

    def arrive(h, dh, dc, side):
        core_ = core if side == 0 else 1 - core
        here = place(h, hi_from[dh], core_, col_from[dc])
        pltpu.make_async_remote_copy(
            src_ref=here,
            dst_ref=here,
            send_sem=send_sems.at[0],
            recv_sem=recv_sems.at[slot_of(h, dh, dc, side)],
            device_id=sibling,
            device_id_type=MESH,
        ).wait_recv()

    for d in range(1, n_hi):
        send(0, 0, 0, {"row": hi_peer[d] * 2 + core}, slot_of(0, d, 0, 0))
    for d in range(1, n_col):
        send(1, 0, 0, {"col": col_peer[d]}, slot_of(1, 0, d, 0))
    for d in range(1, n_col):
        send(0, 0, 0, {"col": col_peer[d]}, slot_of(0, 0, d, 0))
    for d in range(1, n_hi):
        send(1, 0, 0, {"row": hi_peer[d] * 2 + core}, slot_of(1, d, 0, 0))
    for h in range(2):
        send(h, 0, 0, sibling, slot_of(h, 0, 0, 1))
    own = pltpu.make_async_copy(
        x_ref,
        out_ref.at[
            pl.ds(MARGIN_RUNS + runs * col, runs),
            pl.ds(pl.multiple_of(MARGIN_ROWS + row * rows, 16), rows),
            :,
        ],
        local_sem,
    )
    own.start()
    lax.fori_loop(0, MARGIN_RUNS, clear_run, 0)
    lax.fori_loop(MARGIN_RUNS, total_runs - MARGIN_RUNS, clear_ends, 0)

    for dh in range(1, n_hi):
        arrive(0, dh, 0, 0)
        for d in range(1, n_col):
            send(0, dh, 0, {"col": col_peer[d]}, slot_of(0, dh, d, 0))
        send(0, dh, 0, sibling, slot_of(0, dh, 0, 1))
    for dc in range(1, n_col):
        arrive(1, 0, dc, 0)
        for d in range(1, n_hi):
            send(1, 0, dc, {"row": hi_peer[d] * 2 + core}, slot_of(1, d, dc, 0))
        send(1, 0, dc, sibling, slot_of(1, 0, dc, 1))
    for dc in range(1, n_col):
        arrive(0, 0, dc, 0)
        send(0, 0, dc, sibling, slot_of(0, 0, dc, 1))
    for dh in range(1, n_hi):
        arrive(1, dh, 0, 0)
        send(1, dh, 0, sibling, slot_of(1, dh, 0, 1))
    for h in range(2):
        for dh in range(1, n_hi):
            for dc in range(1, n_col):
                arrive(h, dh, dc, 0)
                send(h, dh, dc, sibling, slot_of(h, dh, dc, 1))
    for h in range(2):
        for dh in range(n_hi):
            for dc in range(n_col):
                arrive(h, dh, dc, 1)
    own.wait()
    for copy in sent:
        copy.wait_send()


def spread(cells, collective_id):
    n_row, n_col = lax.axis_size("row"), lax.axis_size("col")
    runs, rows, width = cells.shape
    tiles = n_row // 2 * n_col
    shape = (runs * n_col + 2 * MARGIN_RUNS, rows * n_row + 2 * MARGIN_ROWS, width)
    copies = 2 * ((n_row // 2 - 1) + (n_col - 1) * (n_row // 2) + tiles) + 2 * tiles
    return pl.pallas_call(
        functools.partial(spread_kernel, n_row, n_col),
        out_shape=jax.ShapeDtypeStruct(shape, cells.dtype),
        in_specs=[pl.BlockSpec(memory_space=VMEM)],
        out_specs=pl.BlockSpec(memory_space=VMEM),
        scratch_shapes=[
            pltpu.SemaphoreType.DMA,
            pltpu.SemaphoreType.DMA((copies,)),
            pltpu.SemaphoreType.DMA((4 * tiles,)),
        ],
        compiler_params=pltpu.CompilerParams(
            collective_id=collective_id, has_side_effects=True, vmem_limit_bytes=LIMIT
        ),
        name="spread_tiles",
    )(cells)


def tap_of(t):
    tap = jnp.maximum(t - 1, 0)
    branch = jnp.where(t == 0, 0, tap // 9 + 1)
    inner = tap % 9
    down = jnp.where(t == 0, 0, (inner // 3 - 1) * branch)
    across = jnp.where(t == 0, 0, (inner % 3 - 1) * branch)
    return branch, down, across


def forward_kernel(runs, rows, x_ref, wp_ref, w_ref, out_ref, total):
    t = pl.program_id(0)
    branch, down, across = tap_of(t)
    u0 = MARGIN_RUNS + runs * lax.axis_index("col") + across
    y0 = MARGIN_ROWS + rows * lax.axis_index("row") + down * (RATE_STEP * SLOT)
    width = x_ref.shape[-1]
    window = x_ref[pl.ds(u0, runs), pl.ds(pl.multiple_of(y0, 16), rows), :].reshape(
        runs * rows, width
    )
    weight = jnp.where(t == 0, wp_ref[...], w_ref[0])
    part = jnp.dot(window, weight, preferred_element_type=jnp.float32)
    fresh = jnp.logical_or(t == 0, lax.rem(t - 1, 9) == 0)

    @pl.when(fresh)
    def _():
        total[...] = part

    @pl.when(jnp.logical_not(fresh))
    def _():
        total[...] += part

    @pl.when(lax.rem(t, 9) == 0)
    def _():
        used = runs * rows
        out_ref[0, pl.ds(0, used), :] = total[...].astype(out_ref.dtype)
        if out_ref.shape[1] > used:
            out_ref[0, pl.ds(used, out_ref.shape[1] - used), :] = jnp.zeros(
                (out_ref.shape[1] - used, out_ref.shape[2]), out_ref.dtype
            )


def forward(spread_x, point_weight, taps, runs, rows, padded):
    width, out_count = point_weight.shape
    return pl.pallas_call(
        functools.partial(forward_kernel, runs, rows),
        grid=(28,),
        out_shape=jax.ShapeDtypeStruct((4, padded, out_count), jnp.bfloat16),
        in_specs=[
            pl.BlockSpec(memory_space=VMEM),
            pl.BlockSpec(memory_space=VMEM),
            pl.BlockSpec((1, width, out_count), lambda t: (jnp.maximum(t - 1, 0), 0, 0)),
        ],
        out_specs=pl.BlockSpec((1, padded, out_count), lambda t: ((t + 8) // 9, 0, 0)),
        scratch_shapes=[VMEM((runs * rows, out_count), jnp.float32)],
        compiler_params=pltpu.CompilerParams(
            dimension_semantics=("arbitrary",), vmem_limit_bytes=LIMIT
        ),
        name="forward_taps",
    )(spread_x, point_weight, taps)


def middle_kernel(
    n_chan, part_ref, gain_ref, shift_ref, pw_ref, pshift_ref, cot_ref,
    out_ref, project_ref, grad_ref, landed, own, send_sems, recv_sems, send2, recv2, local_sem,
):
    me = lax.axis_index("chan")
    size = cot_ref.shape[0]
    width = gain_ref.shape[1]
    peers = [lax.rem(me + d, n_chan) for d in range(n_chan)]
    froms = [lax.rem(me - d + n_chan, n_chan) for d in range(n_chan)]
    barrier = pltpu.get_barrier_semaphore()
    for d in range(1, n_chan):
        pl.semaphore_signal(barrier, inc=1, device_id={"chan": peers[d]}, device_id_type=MESH)
    pl.semaphore_wait(barrier, n_chan - 1)
    copies = []
    for d in range(1, n_chan):
        copy = pltpu.make_async_remote_copy(
            src_ref=part_ref.at[:, pl.ds(pl.multiple_of(peers[d] * size, 16), size), :],
            dst_ref=landed.at[d - 1],
            send_sem=send_sems.at[d - 1],
            recv_sem=recv_sems.at[d - 1],
            device_id={"chan": peers[d]},
            device_id_type=MESH,
        )
        copy.start()
        copies.append(copy)
    for copy in copies:
        copy.wait_recv()
    acts = []
    mixed = jnp.zeros((size, width), jnp.float32)
    hiddens = []
    mine = pl.ds(pl.multiple_of(me * size, 16), size)
    for b in range(4):
        pre = part_ref[b, mine, :].astype(jnp.float32)
        for d in range(n_chan - 1):
            pre = pre + landed[d, b].astype(jnp.float32)
        act = pre * gain_ref[b][None, :] + shift_ref[b][None, :]
        hidden = (act * jax.nn.sigmoid(act)).astype(jnp.bfloat16)
        acts.append(act)
        hiddens.append(hidden)
        mixed = mixed + jnp.dot(hidden, pw_ref[b], preferred_element_type=jnp.float32)
    mixed_act = mixed + pshift_ref[...]
    logistic = jax.nn.sigmoid(mixed_act)
    out_ref[...] = (mixed_act * logistic).astype(jnp.bfloat16)
    mixed_grad = (
        cot_ref[...].astype(jnp.float32) * (logistic * (1.0 + mixed_act * (1.0 - logistic)))
    ).astype(jnp.bfloat16)
    for b in range(4):
        hidden_grad = lax.dot_general(
            mixed_grad, pw_ref[b], (((1,), (1,)), ((), ())), preferred_element_type=jnp.float32
        )
        own[:, b * width : (b + 1) * width] = (
            hidden_grad * silu_slope(acts[b]) * gain_ref[b][None, :]
        ).astype(jnp.bfloat16)
    place = grad_ref.at[mine, :]
    local = pltpu.make_async_copy(own, place, local_sem)
    local.start()
    grads = []
    for d in range(1, n_chan):
        copy = pltpu.make_async_remote_copy(
            src_ref=own,
            dst_ref=place,
            send_sem=send2.at[d - 1],
            recv_sem=recv2.at[d - 1],
            device_id={"chan": peers[d]},
            device_id_type=MESH,
        )
        copy.start()
        grads.append(copy)
    for b in range(4):
        project_ref[b] = lax.dot_general(
            hiddens[b], mixed_grad, (((0,), (0,)), ((), ())), preferred_element_type=jnp.float32
        )
    local.wait()
    for d in range(1, n_chan):
        there = grad_ref.at[pl.ds(pl.multiple_of(froms[d] * size, 16), size), :]
        pltpu.make_async_remote_copy(
            src_ref=own,
            dst_ref=there,
            send_sem=send2.at[d - 1],
            recv_sem=recv2.at[d - 1],
            device_id={"chan": peers[d]},
            device_id_type=MESH,
        ).wait_recv()
    for copy in copies + grads:
        copy.wait_send()


def middle(part, gain, shift, pw, pshift, cot):
    n_chan = lax.axis_size("chan")
    size, width = cot.shape
    vmem = pl.BlockSpec(memory_space=VMEM)
    dma = pltpu.SemaphoreType.DMA((n_chan - 1,))
    return pl.pallas_call(
        functools.partial(middle_kernel, n_chan),
        out_shape=(
            jax.ShapeDtypeStruct((size, width), jnp.bfloat16),
            jax.ShapeDtypeStruct((4, width, width), jnp.float32),
            jax.ShapeDtypeStruct((size * n_chan, 4 * width), jnp.bfloat16),
        ),
        in_specs=[vmem] * 6,
        out_specs=(vmem,) * 3,
        scratch_shapes=[
            VMEM((n_chan - 1, 4, size, width), jnp.bfloat16),
            VMEM((size, 4 * width), jnp.bfloat16),
            dma, dma, dma, dma,
            pltpu.SemaphoreType.DMA,
        ],
        compiler_params=pltpu.CompilerParams(
            collective_id=2, has_side_effects=True, vmem_limit_bytes=LIMIT
        ),
        name="middle",
    )(part, gain, shift, pw, pshift, cot)


def backward_kernel(runs, rows, xt_ref, b_ref, wp_ref, w_ref, point_ref, dil_ref, in_ref, total, grad):
    t = pl.program_id(0)
    branch, down, across = tap_of(t)
    pairs, width, depth = xt_ref.shape
    out_count = b_ref.shape[-1]
    full_rows = b_ref.shape[1] - 2 * MARGIN_ROWS
    y_off = pl.multiple_of(MARGIN_ROWS - down * (RATE_STEP * SLOT), 16)

    def step(g, _):
        cells = b_ref[pl.ds(MARGIN_RUNS - across + 2 * g, 2), pl.ds(y_off, full_rows), :]
        part = jnp.dot(
            xt_ref[g], cells.reshape(depth, out_count), preferred_element_type=jnp.float32
        )

        @pl.when(g == 0)
        def _():
            grad[...] = part

        @pl.when(g > 0)
        def _():
            grad[...] += part

        return 0

    lax.fori_loop(0, pairs, step, 0)

    @pl.when(t == 0)
    def _():
        point_ref[...] = grad[...].astype(jnp.bfloat16)

    @pl.when(t > 0)
    def _():
        dil_ref[0] = grad[...].astype(jnp.bfloat16)

    u0 = MARGIN_RUNS + runs * lax.axis_index("col") - across
    y0 = MARGIN_ROWS + rows * lax.axis_index("row") - down * (RATE_STEP * SLOT)
    window = b_ref[pl.ds(u0, runs), pl.ds(pl.multiple_of(y0, 16), rows), :].reshape(
        runs * rows, out_count
    )
    weight = jnp.where(t == 0, wp_ref[...], w_ref[0])
    part = lax.dot_general(
        window, weight, (((1,), (1,)), ((), ())), preferred_element_type=jnp.float32
    )

    @pl.when(t == 0)
    def _():
        total[...] = part

    @pl.when(t > 0)
    def _():
        total[...] += part

    @pl.when(t == 27)
    def _():
        in_ref[...] = total[...].astype(jnp.bfloat16)


def backward(xt, spread_b, point_weight, taps, runs, rows):
    width, out_count = point_weight.shape
    total_runs, total_rows, _ = spread_b.shape
    tap_index = lambda t: (jnp.maximum(t - 1, 0), 0, 0)
    return pl.pallas_call(
        functools.partial(backward_kernel, runs, rows),
        grid=(28,),
        out_shape=(
            jax.ShapeDtypeStruct((width, out_count), jnp.bfloat16),
            jax.ShapeDtypeStruct((27, width, out_count), jnp.bfloat16),
            jax.ShapeDtypeStruct((runs * rows, width), jnp.bfloat16),
        ),
        in_specs=[
            pl.BlockSpec(memory_space=VMEM),
            pl.BlockSpec((total_runs, total_rows, out_count), lambda t: (0, 0, (t + 8) // 9)),
            pl.BlockSpec(memory_space=VMEM),
            pl.BlockSpec((1, width, out_count), tap_index),
        ],
        out_specs=(
            pl.BlockSpec((width, out_count), lambda t: (0, 0)),
            pl.BlockSpec((1, width, out_count), tap_index),
            pl.BlockSpec((runs * rows, width), lambda t: (0, 0)),
        ),
        scratch_shapes=[
            VMEM((runs * rows, width), jnp.float32),
            VMEM((width, out_count), jnp.float32),
        ],
        compiler_params=pltpu.CompilerParams(
            dimension_semantics=("arbitrary",), vmem_limit_bytes=LIMIT
        ),
        name="backward_taps",
    )(xt, spread_b, point_weight, taps)


def per_device(
    features,
    dilated_weight,
    point_weight,
    branch_gain,
    branch_shift,
    project_weight,
    project_shift,
    cotangent,
):
    local_in, tile_h, tile_w = features.shape
    out_count = point_weight.shape[1]
    local_out = branch_gain.shape[0]
    n_chan = lax.axis_size("chan")
    me = lax.axis_index("chan")
    runs, rows = tile_w // RATE_STEP, tile_h * SLOT
    used = runs * rows
    size = (-(-used // n_chan) + 15) // 16 * 16
    padded = size * n_chan
    taps = dilated_weight.reshape(27, local_in, out_count)

    spread_x = spread(to_runs(features), 0)
    vectors = jnp.concatenate([branch_gain, branch_shift, project_shift[:, None]], axis=1)
    vectors = lax.all_gather(vectors, "chan", axis=0, tiled=True).T
    gain, shift, pshift = vectors[:4], vectors[4:8], vectors[8:9]
    pw = lax.all_gather(project_weight, "chan", axis=0, tiled=True).transpose(1, 0, 2)
    cot = to_runs(cotangent).reshape(used, local_out)
    cot = jnp.pad(cot, ((0, padded - used), (0, 0)))
    cot = lax.all_to_all(cot, "chan", split_axis=0, concat_axis=1, tiled=True)

    part = forward(spread_x, point_weight, taps, runs, rows, padded)
    mixed_out, project, grads = middle(part, gain, shift, pw, pshift, cot)
    spread_b = spread(grads[:used].reshape(runs, rows, 4 * out_count), 1)

    total_runs, total_rows, _ = spread_x.shape
    inner = spread_x[MARGIN_RUNS:-MARGIN_RUNS, MARGIN_ROWS:-MARGIN_ROWS]
    pairs = inner.shape[0] // 2
    xt = inner.reshape(pairs, 2 * inner.shape[1], local_in).transpose(0, 2, 1)
    point_grad, dilated_grad, input_grad = backward(
        xt, spread_b, point_weight, taps, runs, rows
    )

    mixed_out = lax.all_to_all(mixed_out, "chan", split_axis=1, concat_axis=0, tiled=True)
    mixed_out = from_runs(mixed_out[:used], tile_h, tile_w)
    project = lax.psum_scatter(project, "chan", scatter_dimension=1, tiled=True)
    project = lax.psum(project, ("row", "col")).astype(jnp.bfloat16).transpose(1, 0, 2)
    return (
        mixed_out,
        from_runs(input_grad, tile_h, tile_w),
        dilated_grad.reshape(dilated_weight.shape),
        point_grad,
        project,
    )


def solution(mesh):
    placed = (
        P("chan", "row", "col"),
        P(None, None, None, "chan", None),
        P("chan", None),
        P("chan", None),
        P("chan", None),
        P("chan", None, None),
        P("chan"),
        P("chan", "row", "col"),
    )
    return jax.shard_map(
        per_device,
        mesh=mesh,
        in_specs=placed,
        out_specs=(
            P("chan", "row", "col"),
            P("chan", "row", "col"),
            P(None, None, None, "chan", None),
            P("chan", None),
            P("chan", None, None),
        ),
        check_vma=False,
    )
```

```python
import functools

import jax
import jax.numpy as jnp
from jax import lax
from jax.experimental import pallas as pl
from jax.experimental.pallas import tpu as pltpu
from jax.sharding import PartitionSpec as P

RATE_STEP = 6
SLOT = 8
MARGIN_RUNS = 3
MARGIN_ROWS = 3 * RATE_STEP * SLOT
MESH = pl.DeviceIdType.MESH
VMEM = pltpu.VMEM
LIMIT = 67_000_000


def silu_slope(values):
    logistic = jax.nn.sigmoid(values)
    return logistic * (1.0 + values * (1.0 - logistic))


def to_runs(cells):
    count, tile_h, tile_w = cells.shape
    runs = tile_w // RATE_STEP
    cells = cells.reshape(count, tile_h, runs, RATE_STEP)
    cells = jnp.pad(cells, ((0, 0), (0, 0), (0, 0), (0, SLOT - RATE_STEP)))
    return cells.transpose(2, 1, 3, 0).reshape(runs, tile_h * SLOT, count)


def from_runs(cells, tile_h, tile_w):
    runs = tile_w // RATE_STEP
    count = cells.shape[-1]
    cells = cells.reshape(runs, tile_h, SLOT, count)[:, :, :RATE_STEP]
    return cells.transpose(3, 1, 0, 2).reshape(count, tile_h, tile_w)


def spread_kernel(n_row, n_col, n_chan, n_extra, summed, *refs):
    x_ref, extras, refs = refs[0], refs[1 : 1 + n_extra], refs[1 + n_extra :]
    if summed:
        project_ref, refs = refs[0], refs[1:]
    out_ref, gathered, refs = refs[0], refs[1 : 1 + n_extra], refs[1 + n_extra :]
    if summed:
        project_out, refs = refs[0], refs[1:]
    local_sem, send_sems, recv_sems, extra_local, extra_send, extra_recv = refs[:6]
    if summed:
        stages, sum_local, sum_send, sum_recv = refs[6:13], refs[13], refs[14], refs[15]
    n_hi = n_row // 2
    chan = lax.axis_index("chan")
    chan_peer = [lax.rem(chan + d, n_chan) for d in range(n_chan)]
    chan_from = [lax.rem(chan - d + n_chan, n_chan) for d in range(n_chan)]
    row = lax.axis_index("row")
    col = lax.axis_index("col")
    hi, core = row // 2, row % 2
    runs, rows, _ = x_ref.shape
    first = (rows // 2 + 15) // 16 * 16
    starts, sizes = (0, first), (first, rows - first)

    hi_peer = [lax.rem(hi + d, n_hi) for d in range(n_hi)]
    hi_from = [lax.rem(hi - d + n_hi, n_hi) for d in range(n_hi)]
    col_peer = [lax.rem(col + d, n_col) for d in range(n_col)]
    col_from = [lax.rem(col - d + n_col, n_col) for d in range(n_col)]
    sibling = {"row": hi * 2 + 1 - core}
    partners = [sibling]
    partners += [{"row": hi_peer[d] * 2 + core} for d in range(1, n_hi)]
    partners += [{"col": col_peer[d]} for d in range(1, n_col)]
    partners += [{"chan": chan_peer[d]} for d in range(1, n_chan)]

    barrier = pltpu.get_barrier_semaphore()
    for who in partners:
        pl.semaphore_signal(barrier, inc=1, device_id=who, device_id_type=MESH)

    dtype = out_ref.dtype
    total_runs, total_rows, width = out_ref.shape
    edge = jnp.zeros((MARGIN_ROWS, width), dtype)

    def clear_run(u, _):
        for at in (u, total_runs - MARGIN_RUNS + u):
            for y in range(0, total_rows, MARGIN_ROWS):
                out_ref[at, pl.ds(y, MARGIN_ROWS), :] = edge
        return 0

    def clear_ends(u, _):
        out_ref[u, pl.ds(0, MARGIN_ROWS), :] = edge
        out_ref[u, pl.ds(total_rows - MARGIN_ROWS, MARGIN_ROWS), :] = edge
        return 0

    pl.semaphore_wait(barrier, len(partners))

    def place(h, hi_, core_, col_):
        return out_ref.at[
            pl.ds(MARGIN_RUNS + runs * col_, runs),
            pl.ds(pl.multiple_of(MARGIN_ROWS + (hi_ * 2 + core_) * rows + starts[h], 16), sizes[h]),
            :,
        ]

    sent = []

    def send(h, dh, dc, who, slot):
        if dh == 0 and dc == 0:
            src = x_ref.at[:, pl.ds(starts[h], sizes[h]), :]
        else:
            src = place(h, hi_from[dh], core, col_from[dc])
        copy = pltpu.make_async_remote_copy(
            src_ref=src,
            dst_ref=place(h, hi_from[dh], core, col_from[dc]),
            send_sem=send_sems.at[len(sent)],
            recv_sem=recv_sems.at[slot],
            device_id=who,
            device_id_type=MESH,
        )
        copy.start()
        sent.append(copy)

    def slot_of(h, dh, dc, side):
        return ((h * n_hi + dh) * n_col + dc) * 2 + side

    def arrive(h, dh, dc, side):
        core_ = core if side == 0 else 1 - core
        here = place(h, hi_from[dh], core_, col_from[dc])
        pltpu.make_async_remote_copy(
            src_ref=here,
            dst_ref=here,
            send_sem=send_sems.at[0],
            recv_sem=recv_sems.at[slot_of(h, dh, dc, side)],
            device_id=sibling,
            device_id_type=MESH,
        ).wait_recv()

    later = []

    def exchange(sources, landing, at, who, local, sends, recvs, base):
        keep = pltpu.make_async_copy(sources[0], landing.at[at], local)
        keep.start()
        for d in range(1, len(sources)):
            copy = pltpu.make_async_remote_copy(
                src_ref=sources[d],
                dst_ref=landing.at[at],
                send_sem=sends.at[base + d - 1],
                recv_sem=recvs.at[base + d - 1],
                device_id=who[d],
                device_id_type=MESH,
            )
            copy.start()
            later.append(copy)

        def finish(froms):
            keep.wait()
            for d in range(1, len(sources)):
                pltpu.make_async_remote_copy(
                    src_ref=landing.at[froms[d]],
                    dst_ref=landing.at[froms[d]],
                    send_sem=sends.at[base + d - 1],
                    recv_sem=recvs.at[base + d - 1],
                    device_id=who[d],
                    device_id_type=MESH,
                ).wait_recv()

        return finish

    chan_who = [{"chan": chan_peer[d]} for d in range(n_chan)]
    for d in range(1, n_hi):
        send(0, 0, 0, {"row": hi_peer[d] * 2 + core}, slot_of(0, d, 0, 0))
    for d in range(1, n_col):
        send(1, 0, 0, {"col": col_peer[d]}, slot_of(1, 0, d, 0))
    if summed:
        slab = project_ref.shape[1] // n_chan
        slabs = [
            project_ref.at[:, pl.ds(pl.multiple_of(chan_peer[d] * slab, 8), slab), :]
            for d in range(n_chan)
        ]
        finish_sum = exchange(
            slabs, stages[0], chan, chan_who, sum_local.at[0], sum_send, sum_recv, 0
        )
        hi_who = [{"row": hi_peer[d] * 2 + core} for d in range(n_hi)]
        col_who = [{"col": col_peer[d]} for d in range(n_col)]
        core_who = [sibling, sibling]

    def total_of(stage, count):
        value = stage[0].astype(jnp.float32)
        for i in range(1, count):
            value = value + stage[i].astype(jnp.float32)
        return value

    finish_extras = [
        exchange(
            [extras[i]] * n_chan, gathered[i], chan, chan_who,
            extra_local.at[i], extra_send, extra_recv, i * (n_chan - 1),
        )
        for i in range(n_extra)
    ]
    for d in range(1, n_col):
        send(0, 0, 0, {"col": col_peer[d]}, slot_of(0, 0, d, 0))
    for d in range(1, n_hi):
        send(1, 0, 0, {"row": hi_peer[d] * 2 + core}, slot_of(1, d, 0, 0))
    for h in range(2):
        send(h, 0, 0, sibling, slot_of(h, 0, 0, 1))
    own = pltpu.make_async_copy(
        x_ref,
        out_ref.at[
            pl.ds(MARGIN_RUNS + runs * col, runs),
            pl.ds(pl.multiple_of(MARGIN_ROWS + row * rows, 16), rows),
            :,
        ],
        local_sem,
    )
    own.start()
    lax.fori_loop(0, MARGIN_RUNS, clear_run, 0)
    lax.fori_loop(MARGIN_RUNS, total_runs - MARGIN_RUNS, clear_ends, 0)

    for dh in range(1, n_hi):
        arrive(0, dh, 0, 0)
        for d in range(1, n_col):
            send(0, dh, 0, {"col": col_peer[d]}, slot_of(0, dh, d, 0))
        send(0, dh, 0, sibling, slot_of(0, dh, 0, 1))
    for dc in range(1, n_col):
        arrive(1, 0, dc, 0)
        for d in range(1, n_hi):
            send(1, 0, dc, {"row": hi_peer[d] * 2 + core}, slot_of(1, d, dc, 0))
        send(1, 0, dc, sibling, slot_of(1, 0, dc, 1))
    if summed:
        finish_sum(chan_from)
        ready = stages[4]
        ready[...] = total_of(stages[0], n_chan).astype(ready.dtype)
        finish_sum = exchange(
            [ready] * n_hi, stages[1], hi, hi_who, sum_local.at[1], sum_send, sum_recv, n_chan - 1
        )
    for dc in range(1, n_col):
        arrive(0, 0, dc, 0)
        send(0, 0, dc, sibling, slot_of(0, 0, dc, 1))
    for dh in range(1, n_hi):
        arrive(1, dh, 0, 0)
        send(1, dh, 0, sibling, slot_of(1, dh, 0, 1))
    if summed:
        finish_sum(hi_from)
        ready = stages[5]
        ready[...] = total_of(stages[1], n_hi).astype(ready.dtype)
        finish_sum = exchange(
            [ready] * n_col, stages[2], col, col_who, sum_local.at[2],
            sum_send, sum_recv, n_chan + n_hi - 2,
        )
    for h in range(2):
        for dh in range(1, n_hi):
            for dc in range(1, n_col):
                arrive(h, dh, dc, 0)
                send(h, dh, dc, sibling, slot_of(h, dh, dc, 1))
    if summed:
        finish_sum(col_from)
        ready = stages[6]
        ready[...] = total_of(stages[2], n_col)
        finish_sum = exchange(
            [ready] * 2, stages[3], core, core_who, sum_local.at[3],
            sum_send, sum_recv, n_chan + n_hi + n_col - 3,
        )
    for h in range(2):
        for dh in range(n_hi):
            for dc in range(n_col):
                arrive(h, dh, dc, 1)
    if summed:
        finish_sum([core, 1 - core])
        project_out[...] = total_of(stages[3], 2).astype(project_out.dtype)
    for finish in finish_extras:
        finish(chan_from)
    for copy in later:
        copy.wait_send()
    own.wait()
    for copy in sent:
        copy.wait_send()


def spread(cells, extras, project, collective_id):
    n_row, n_col, n_chan = (lax.axis_size(axis) for axis in ("row", "col", "chan"))
    n_hi = n_row // 2
    runs, rows, width = cells.shape
    tiles = n_hi * n_col
    shape = (runs * n_col + 2 * MARGIN_RUNS, rows * n_row + 2 * MARGIN_ROWS, width)
    copies = 2 * ((n_hi - 1) + (n_col - 1) * n_hi + tiles) + 2 * tiles
    vmem = pl.BlockSpec(memory_space=VMEM)
    dma = pltpu.SemaphoreType.DMA
    operands = [cells, *extras]
    outs = [jax.ShapeDtypeStruct(shape, cells.dtype)]
    outs += [jax.ShapeDtypeStruct((n_chan, *e.shape), e.dtype) for e in extras]
    scratch = [
        dma,
        dma((copies,)),
        dma((4 * tiles,)),
        dma((len(extras),)),
        dma((len(extras) * (n_chan - 1),)),
        dma((len(extras) * (n_chan - 1),)),
    ]
    if project is not None:
        slab = (project.shape[0], project.shape[1] // n_chan, project.shape[2])
        operands.append(project)
        outs.append(jax.ShapeDtypeStruct(slab, jnp.bfloat16))
        peers = n_chan + n_hi + n_col - 2
        scratch += [
            VMEM((n_chan, *slab), jnp.float32),
            VMEM((n_hi, *slab), jnp.bfloat16),
            VMEM((n_col, *slab), jnp.bfloat16),
            VMEM((2, *slab), jnp.float32),
            VMEM(slab, jnp.bfloat16),
            VMEM(slab, jnp.bfloat16),
            VMEM(slab, jnp.float32),
            dma((4,)),
            dma((peers,)),
            dma((peers,)),
        ]
    body = functools.partial(
        spread_kernel, n_row, n_col, n_chan, len(extras), project is not None
    )
    return pl.pallas_call(
        body,
        out_shape=tuple(outs),
        in_specs=[vmem] * len(operands),
        out_specs=(vmem,) * len(outs),
        scratch_shapes=scratch,
        compiler_params=pltpu.CompilerParams(
            collective_id=collective_id, has_side_effects=True, vmem_limit_bytes=LIMIT
        ),
        name="spread_tiles",
    )(*operands)


def tap_of(t):
    tap = jnp.maximum(t - 1, 0)
    branch = jnp.where(t == 0, 0, tap // 9 + 1)
    inner = tap % 9
    down = jnp.where(t == 0, 0, (inner // 3 - 1) * branch)
    across = jnp.where(t == 0, 0, (inner % 3 - 1) * branch)
    return branch, down, across


def forward_kernel(runs, rows, x_ref, wp_ref, w_ref, out_ref, total):
    t = pl.program_id(0)
    branch, down, across = tap_of(t)
    u0 = MARGIN_RUNS + runs * lax.axis_index("col") + across
    y0 = MARGIN_ROWS + rows * lax.axis_index("row") + down * (RATE_STEP * SLOT)
    width = x_ref.shape[-1]
    window = x_ref[pl.ds(u0, runs), pl.ds(pl.multiple_of(y0, 16), rows), :].reshape(
        runs * rows, width
    )
    weight = jnp.where(t == 0, wp_ref[...], w_ref[0])
    part = jnp.dot(window, weight, preferred_element_type=jnp.float32)
    fresh = jnp.logical_or(t == 0, lax.rem(t - 1, 9) == 0)

    @pl.when(fresh)
    def _():
        total[...] = part

    @pl.when(jnp.logical_not(fresh))
    def _():
        total[...] += part

    @pl.when(lax.rem(t, 9) == 0)
    def _():
        used = runs * rows
        out_ref[0, pl.ds(0, used), :] = total[...].astype(out_ref.dtype)
        if out_ref.shape[1] > used:
            out_ref[0, pl.ds(used, out_ref.shape[1] - used), :] = jnp.zeros(
                (out_ref.shape[1] - used, out_ref.shape[2]), out_ref.dtype
            )


def forward(spread_x, point_weight, taps, runs, rows, padded):
    width, out_count = point_weight.shape
    return pl.pallas_call(
        functools.partial(forward_kernel, runs, rows),
        grid=(28,),
        out_shape=jax.ShapeDtypeStruct((4, padded, out_count), jnp.bfloat16),
        in_specs=[
            pl.BlockSpec(memory_space=VMEM),
            pl.BlockSpec(memory_space=VMEM),
            pl.BlockSpec((1, width, out_count), lambda t: (jnp.maximum(t - 1, 0), 0, 0)),
        ],
        out_specs=pl.BlockSpec((1, padded, out_count), lambda t: ((t + 8) // 9, 0, 0)),
        scratch_shapes=[VMEM((runs * rows, out_count), jnp.float32)],
        compiler_params=pltpu.CompilerParams(
            dimension_semantics=("arbitrary",), vmem_limit_bytes=LIMIT
        ),
        name="forward_taps",
    )(spread_x, point_weight, taps)


def middle_kernel(
    n_chan, part_ref, gain_ref, shift_ref, pw_ref, pshift_ref, cot_ref,
    out_ref, project_ref, grad_ref, landed, own, send_sems, recv_sems, send2, recv2, local_sem,
):
    me = lax.axis_index("chan")
    size = cot_ref.shape[0]
    width = gain_ref.shape[1]
    peers = [lax.rem(me + d, n_chan) for d in range(n_chan)]
    froms = [lax.rem(me - d + n_chan, n_chan) for d in range(n_chan)]
    barrier = pltpu.get_barrier_semaphore()
    for d in range(1, n_chan):
        pl.semaphore_signal(barrier, inc=1, device_id={"chan": peers[d]}, device_id_type=MESH)
    pl.semaphore_wait(barrier, n_chan - 1)
    copies = []
    for d in range(1, n_chan):
        copy = pltpu.make_async_remote_copy(
            src_ref=part_ref.at[:, pl.ds(pl.multiple_of(peers[d] * size, 16), size), :],
            dst_ref=landed.at[d - 1],
            send_sem=send_sems.at[d - 1],
            recv_sem=recv_sems.at[d - 1],
            device_id={"chan": peers[d]},
            device_id_type=MESH,
        )
        copy.start()
        copies.append(copy)
    for copy in copies:
        copy.wait_recv()
    acts = []
    mixed = jnp.zeros((size, width), jnp.float32)
    hiddens = []
    mine = pl.ds(pl.multiple_of(me * size, 16), size)
    for b in range(4):
        pre = part_ref[b, mine, :].astype(jnp.float32)
        for d in range(n_chan - 1):
            pre = pre + landed[d, b].astype(jnp.float32)
        act = pre * gain_ref[b][None, :] + shift_ref[b][None, :]
        hidden = (act * jax.nn.sigmoid(act)).astype(jnp.bfloat16)
        acts.append(act)
        hiddens.append(hidden)
        mixed = mixed + jnp.dot(hidden, pw_ref[b], preferred_element_type=jnp.float32)
    mixed_act = mixed + pshift_ref[...]
    logistic = jax.nn.sigmoid(mixed_act)
    out_ref[...] = (mixed_act * logistic).astype(jnp.bfloat16)
    mixed_grad = (
        cot_ref[...].astype(jnp.float32) * (logistic * (1.0 + mixed_act * (1.0 - logistic)))
    ).astype(jnp.bfloat16)
    for b in range(4):
        hidden_grad = lax.dot_general(
            mixed_grad, pw_ref[b], (((1,), (1,)), ((), ())), preferred_element_type=jnp.float32
        )
        own[:, b * width : (b + 1) * width] = (
            hidden_grad * silu_slope(acts[b]) * gain_ref[b][None, :]
        ).astype(jnp.bfloat16)
    place = grad_ref.at[mine, :]
    local = pltpu.make_async_copy(own, place, local_sem)
    local.start()
    grads = []
    for d in range(1, n_chan):
        copy = pltpu.make_async_remote_copy(
            src_ref=own,
            dst_ref=place,
            send_sem=send2.at[d - 1],
            recv_sem=recv2.at[d - 1],
            device_id={"chan": peers[d]},
            device_id_type=MESH,
        )
        copy.start()
        grads.append(copy)
    for b in range(4):
        project_ref[b] = lax.dot_general(
            hiddens[b], mixed_grad, (((0,), (0,)), ((), ())), preferred_element_type=jnp.float32
        )
    local.wait()
    for d in range(1, n_chan):
        there = grad_ref.at[pl.ds(pl.multiple_of(froms[d] * size, 16), size), :]
        pltpu.make_async_remote_copy(
            src_ref=own,
            dst_ref=there,
            send_sem=send2.at[d - 1],
            recv_sem=recv2.at[d - 1],
            device_id={"chan": peers[d]},
            device_id_type=MESH,
        ).wait_recv()
    for copy in copies + grads:
        copy.wait_send()


def middle(part, gain, shift, pw, pshift, cot):
    n_chan = lax.axis_size("chan")
    size, width = cot.shape
    vmem = pl.BlockSpec(memory_space=VMEM)
    dma = pltpu.SemaphoreType.DMA((n_chan - 1,))
    return pl.pallas_call(
        functools.partial(middle_kernel, n_chan),
        out_shape=(
            jax.ShapeDtypeStruct((size, width), jnp.bfloat16),
            jax.ShapeDtypeStruct((4, width, width), jnp.float32),
            jax.ShapeDtypeStruct((size * n_chan, 4 * width), jnp.bfloat16),
        ),
        in_specs=[vmem] * 6,
        out_specs=(vmem,) * 3,
        scratch_shapes=[
            VMEM((n_chan - 1, 4, size, width), jnp.bfloat16),
            VMEM((size, 4 * width), jnp.bfloat16),
            dma, dma, dma, dma,
            pltpu.SemaphoreType.DMA,
        ],
        compiler_params=pltpu.CompilerParams(
            collective_id=2, has_side_effects=True, vmem_limit_bytes=LIMIT
        ),
        name="middle",
    )(part, gain, shift, pw, pshift, cot)


def backward_kernel(runs, rows, xt_ref, b_ref, wp_ref, w_ref, point_ref, dil_ref, in_ref, total, grad):
    t = pl.program_id(0)
    branch, down, across = tap_of(t)
    pairs, width, depth = xt_ref.shape
    out_count = b_ref.shape[-1]
    full_rows = b_ref.shape[1] - 2 * MARGIN_ROWS
    y_off = pl.multiple_of(MARGIN_ROWS - down * (RATE_STEP * SLOT), 16)

    def step(g, _):
        cells = b_ref[pl.ds(MARGIN_RUNS - across + 2 * g, 2), pl.ds(y_off, full_rows), :]
        part = jnp.dot(
            xt_ref[g], cells.reshape(depth, out_count), preferred_element_type=jnp.float32
        )

        @pl.when(g == 0)
        def _():
            grad[...] = part

        @pl.when(g > 0)
        def _():
            grad[...] += part

        return 0

    lax.fori_loop(0, pairs, step, 0)

    @pl.when(t == 0)
    def _():
        point_ref[...] = grad[...].astype(jnp.bfloat16)

    @pl.when(t > 0)
    def _():
        dil_ref[0] = grad[...].astype(jnp.bfloat16)

    u0 = MARGIN_RUNS + runs * lax.axis_index("col") - across
    y0 = MARGIN_ROWS + rows * lax.axis_index("row") - down * (RATE_STEP * SLOT)
    window = b_ref[pl.ds(u0, runs), pl.ds(pl.multiple_of(y0, 16), rows), :].reshape(
        runs * rows, out_count
    )
    weight = jnp.where(t == 0, wp_ref[...], w_ref[0])
    part = lax.dot_general(
        window, weight, (((1,), (1,)), ((), ())), preferred_element_type=jnp.float32
    )

    @pl.when(t == 0)
    def _():
        total[...] = part

    @pl.when(t > 0)
    def _():
        total[...] += part

    @pl.when(t == 27)
    def _():
        in_ref[...] = total[...].astype(jnp.bfloat16)


def backward(xt, spread_b, point_weight, taps, runs, rows):
    width, out_count = point_weight.shape
    total_runs, total_rows, _ = spread_b.shape
    tap_index = lambda t: (jnp.maximum(t - 1, 0), 0, 0)
    return pl.pallas_call(
        functools.partial(backward_kernel, runs, rows),
        grid=(28,),
        out_shape=(
            jax.ShapeDtypeStruct((width, out_count), jnp.bfloat16),
            jax.ShapeDtypeStruct((27, width, out_count), jnp.bfloat16),
            jax.ShapeDtypeStruct((runs * rows, width), jnp.bfloat16),
        ),
        in_specs=[
            pl.BlockSpec(memory_space=VMEM),
            pl.BlockSpec((total_runs, total_rows, out_count), lambda t: (0, 0, (t + 8) // 9)),
            pl.BlockSpec(memory_space=VMEM),
            pl.BlockSpec((1, width, out_count), tap_index),
        ],
        out_specs=(
            pl.BlockSpec((width, out_count), lambda t: (0, 0)),
            pl.BlockSpec((1, width, out_count), tap_index),
            pl.BlockSpec((runs * rows, width), lambda t: (0, 0)),
        ),
        scratch_shapes=[
            VMEM((runs * rows, width), jnp.float32),
            VMEM((width, out_count), jnp.float32),
        ],
        compiler_params=pltpu.CompilerParams(
            dimension_semantics=("arbitrary",), vmem_limit_bytes=LIMIT
        ),
        name="backward_taps",
    )(xt, spread_b, point_weight, taps)


def per_device(
    features,
    dilated_weight,
    point_weight,
    branch_gain,
    branch_shift,
    project_weight,
    project_shift,
    cotangent,
):
    local_in, tile_h, tile_w = features.shape
    out_count = point_weight.shape[1]
    local_out = branch_gain.shape[0]
    n_chan = lax.axis_size("chan")
    me = lax.axis_index("chan")
    runs, rows = tile_w // RATE_STEP, tile_h * SLOT
    used = runs * rows
    size = (-(-used // n_chan) + 15) // 16 * 16
    padded = size * n_chan
    taps = dilated_weight.reshape(27, local_in, out_count)

    vectors = jnp.concatenate([branch_gain, branch_shift, project_shift[:, None]], axis=1)
    cot = to_runs(cotangent).reshape(used, local_out)
    cot = jnp.pad(cot, ((0, padded - used), (0, 0)))
    spread_x, vectors, pw, cot = spread(
        to_runs(features), [vectors, project_weight.transpose(1, 0, 2), cot], None, 0
    )
    vectors = vectors.transpose(2, 0, 1).reshape(9, out_count)
    gain, shift, pshift = vectors[:4], vectors[4:8], vectors[8:9]
    pw = pw.transpose(1, 0, 2, 3).reshape(4, out_count, out_count)
    cot = lax.dynamic_slice_in_dim(cot, me * size, size, axis=1)
    cot = cot.transpose(1, 0, 2).reshape(size, out_count)

    part = forward(spread_x, point_weight, taps, runs, rows, padded)
    mixed_out, project, grads = middle(part, gain, shift, pw, pshift, cot)
    spread_b, mixed_out, project = spread(
        grads[:used].reshape(runs, rows, 4 * out_count), [mixed_out], project, 1
    )

    total_runs, total_rows, _ = spread_x.shape
    inner = spread_x[MARGIN_RUNS:-MARGIN_RUNS, MARGIN_ROWS:-MARGIN_ROWS]
    pairs = inner.shape[0] // 2
    xt = inner.reshape(pairs, 2 * inner.shape[1], local_in).transpose(0, 2, 1)
    point_grad, dilated_grad, input_grad = backward(
        xt, spread_b, point_weight, taps, runs, rows
    )

    mixed_out = lax.dynamic_slice_in_dim(mixed_out, me * local_out, local_out, axis=2)
    mixed_out = from_runs(mixed_out.reshape(padded, local_out)[:used], tile_h, tile_w)
    return (
        mixed_out,
        from_runs(input_grad, tile_h, tile_w),
        dilated_grad.reshape(dilated_weight.shape),
        point_grad,
        project.transpose(1, 0, 2),
    )


def solution(mesh):
    placed = (
        P("chan", "row", "col"),
        P(None, None, None, "chan", None),
        P("chan", None),
        P("chan", None),
        P("chan", None),
        P("chan", None, None),
        P("chan"),
        P("chan", "row", "col"),
    )
    return jax.shard_map(
        per_device,
        mesh=mesh,
        in_specs=placed,
        out_specs=(
            P("chan", "row", "col"),
            P("chan", "row", "col"),
            P(None, None, None, "chan", None),
            P("chan", None),
            P("chan", None, None),
        ),
        check_vma=False,
    )
```

```python
import functools

import jax
import jax.numpy as jnp
from jax import lax
from jax.experimental import pallas as pl
from jax.experimental.pallas import tpu as pltpu
from jax.sharding import PartitionSpec as P

RATE_STEP = 6
SLOT = 8
MARGIN_RUNS = 3
MARGIN_ROWS = 3 * RATE_STEP * SLOT
MESH = pl.DeviceIdType.MESH
VMEM = pltpu.VMEM
LIMIT = 67_000_000


def silu_slope(values):
    logistic = jax.nn.sigmoid(values)
    return logistic * (1.0 + values * (1.0 - logistic))


def to_runs(cells):
    count, tile_h, tile_w = cells.shape
    runs = tile_w // RATE_STEP
    cells = cells.reshape(count, tile_h, runs, RATE_STEP)
    cells = jnp.pad(cells, ((0, 0), (0, 0), (0, 0), (0, SLOT - RATE_STEP)))
    return cells.transpose(2, 1, 3, 0).reshape(runs, tile_h * SLOT, count)


def from_runs(cells, tile_h, tile_w):
    runs = tile_w // RATE_STEP
    count = cells.shape[-1]
    cells = cells.reshape(runs, tile_h, SLOT, count)[:, :, :RATE_STEP]
    return cells.transpose(3, 1, 0, 2).reshape(count, tile_h, tile_w)


def spread_kernel(n_row, n_col, n_chan, n_extra, summed, *refs):
    x_ref, extras, refs = refs[0], refs[1 : 1 + n_extra], refs[1 + n_extra :]
    if summed:
        project_ref, refs = refs[0], refs[1:]
    out_ref, gathered, refs = refs[0], refs[1 : 1 + n_extra], refs[1 + n_extra :]
    if summed:
        project_out, refs = refs[0], refs[1:]
    local_sem, send_sems, recv_sems, extra_local, extra_send, extra_recv = refs[:6]
    if summed:
        stages, sum_local, sum_send, sum_recv = refs[6:13], refs[13], refs[14], refs[15]
    n_hi = n_row // 2
    chan = lax.axis_index("chan")
    chan_peer = [lax.rem(chan + d, n_chan) for d in range(n_chan)]
    chan_from = [lax.rem(chan - d + n_chan, n_chan) for d in range(n_chan)]
    row = lax.axis_index("row")
    col = lax.axis_index("col")
    hi, core = row // 2, row % 2
    runs, rows, _ = x_ref.shape
    first = (rows // 2 + 15) // 16 * 16
    starts, sizes = (0, first), (first, rows - first)

    hi_peer = [lax.rem(hi + d, n_hi) for d in range(n_hi)]
    hi_from = [lax.rem(hi - d + n_hi, n_hi) for d in range(n_hi)]
    col_peer = [lax.rem(col + d, n_col) for d in range(n_col)]
    col_from = [lax.rem(col - d + n_col, n_col) for d in range(n_col)]
    sibling = {"row": hi * 2 + 1 - core}
    partners = [sibling]
    partners += [{"row": hi_peer[d] * 2 + core} for d in range(1, n_hi)]
    partners += [{"col": col_peer[d]} for d in range(1, n_col)]
    partners += [{"chan": chan_peer[d]} for d in range(1, n_chan)]

    barrier = pltpu.get_barrier_semaphore()
    for who in partners:
        pl.semaphore_signal(barrier, inc=1, device_id=who, device_id_type=MESH)

    dtype = out_ref.dtype
    total_runs, total_rows, width = out_ref.shape
    edge = jnp.zeros((MARGIN_ROWS, width), dtype)

    def clear_run(u, _):
        for at in (u, total_runs - MARGIN_RUNS + u):
            for y in range(0, total_rows, MARGIN_ROWS):
                out_ref[at, pl.ds(y, MARGIN_ROWS), :] = edge
        return 0

    def clear_ends(u, _):
        out_ref[u, pl.ds(0, MARGIN_ROWS), :] = edge
        out_ref[u, pl.ds(total_rows - MARGIN_ROWS, MARGIN_ROWS), :] = edge
        return 0

    pl.semaphore_wait(barrier, len(partners))

    def place(h, hi_, core_, col_):
        return out_ref.at[
            pl.ds(MARGIN_RUNS + runs * col_, runs),
            pl.ds(pl.multiple_of(MARGIN_ROWS + (hi_ * 2 + core_) * rows + starts[h], 16), sizes[h]),
            :,
        ]

    sent = []

    def send(h, dh, dc, who, slot):
        if dh == 0 and dc == 0:
            src = x_ref.at[:, pl.ds(starts[h], sizes[h]), :]
        else:
            src = place(h, hi_from[dh], core, col_from[dc])
        copy = pltpu.make_async_remote_copy(
            src_ref=src,
            dst_ref=place(h, hi_from[dh], core, col_from[dc]),
            send_sem=send_sems.at[len(sent)],
            recv_sem=recv_sems.at[slot],
            device_id=who,
            device_id_type=MESH,
        )
        copy.start()
        sent.append(copy)

    def slot_of(h, dh, dc, side):
        return ((h * n_hi + dh) * n_col + dc) * 2 + side

    def arrive(h, dh, dc, side):
        core_ = core if side == 0 else 1 - core
        here = place(h, hi_from[dh], core_, col_from[dc])
        pltpu.make_async_remote_copy(
            src_ref=here,
            dst_ref=here,
            send_sem=send_sems.at[0],
            recv_sem=recv_sems.at[slot_of(h, dh, dc, side)],
            device_id=sibling,
            device_id_type=MESH,
        ).wait_recv()

    later = []

    def exchange(sources, landing, at, who, local, sends, recvs, base):
        keep = pltpu.make_async_copy(sources[0], landing.at[at], local)
        keep.start()
        for d in range(1, len(sources)):
            copy = pltpu.make_async_remote_copy(
                src_ref=sources[d],
                dst_ref=landing.at[at],
                send_sem=sends.at[base + d - 1],
                recv_sem=recvs.at[base + d - 1],
                device_id=who[d],
                device_id_type=MESH,
            )
            copy.start()
            later.append(copy)

        def finish(froms):
            keep.wait()
            for d in range(1, len(sources)):
                pltpu.make_async_remote_copy(
                    src_ref=landing.at[froms[d]],
                    dst_ref=landing.at[froms[d]],
                    send_sem=sends.at[base + d - 1],
                    recv_sem=recvs.at[base + d - 1],
                    device_id=who[d],
                    device_id_type=MESH,
                ).wait_recv()

        return finish

    chan_who = [{"chan": chan_peer[d]} for d in range(n_chan)]
    for d in range(1, n_hi):
        send(0, 0, 0, {"row": hi_peer[d] * 2 + core}, slot_of(0, d, 0, 0))
    for d in range(1, n_col):
        send(1, 0, 0, {"col": col_peer[d]}, slot_of(1, 0, d, 0))
    if summed:
        slab = project_ref.shape[1] // n_chan
        slabs = [
            project_ref.at[:, pl.ds(pl.multiple_of(chan_peer[d] * slab, 8), slab), :]
            for d in range(n_chan)
        ]
        finish_sum = exchange(
            slabs, stages[0], chan, chan_who, sum_local.at[0], sum_send, sum_recv, 0
        )
        hi_who = [{"row": hi_peer[d] * 2 + core} for d in range(n_hi)]
        col_who = [{"col": col_peer[d]} for d in range(n_col)]
        core_who = [sibling, sibling]

    def total_of(stage, count):
        value = stage[0].astype(jnp.float32)
        for i in range(1, count):
            value = value + stage[i].astype(jnp.float32)
        return value

    finish_extras = [
        exchange(
            [extras[i]] * n_chan, gathered[i], chan, chan_who,
            extra_local.at[i], extra_send, extra_recv, i * (n_chan - 1),
        )
        for i in range(n_extra)
    ]
    for d in range(1, n_col):
        send(0, 0, 0, {"col": col_peer[d]}, slot_of(0, 0, d, 0))
    for d in range(1, n_hi):
        send(1, 0, 0, {"row": hi_peer[d] * 2 + core}, slot_of(1, d, 0, 0))
    for h in range(2):
        send(h, 0, 0, sibling, slot_of(h, 0, 0, 1))
    own = pltpu.make_async_copy(
        x_ref,
        out_ref.at[
            pl.ds(MARGIN_RUNS + runs * col, runs),
            pl.ds(pl.multiple_of(MARGIN_ROWS + row * rows, 16), rows),
            :,
        ],
        local_sem,
    )
    own.start()
    lax.fori_loop(0, MARGIN_RUNS, clear_run, 0)
    lax.fori_loop(MARGIN_RUNS, total_runs - MARGIN_RUNS, clear_ends, 0)

    for dh in range(1, n_hi):
        arrive(0, dh, 0, 0)
        for d in range(1, n_col):
            send(0, dh, 0, {"col": col_peer[d]}, slot_of(0, dh, d, 0))
        send(0, dh, 0, sibling, slot_of(0, dh, 0, 1))
    for dc in range(1, n_col):
        arrive(1, 0, dc, 0)
        for d in range(1, n_hi):
            send(1, 0, dc, {"row": hi_peer[d] * 2 + core}, slot_of(1, d, dc, 0))
        send(1, 0, dc, sibling, slot_of(1, 0, dc, 1))
    if summed:
        finish_sum(chan_from)
        ready = stages[4]
        ready[...] = total_of(stages[0], n_chan).astype(ready.dtype)
        finish_sum = exchange(
            [ready] * n_hi, stages[1], hi, hi_who, sum_local.at[1], sum_send, sum_recv, n_chan - 1
        )
    for dc in range(1, n_col):
        arrive(0, 0, dc, 0)
        send(0, 0, dc, sibling, slot_of(0, 0, dc, 1))
    for dh in range(1, n_hi):
        arrive(1, dh, 0, 0)
        send(1, dh, 0, sibling, slot_of(1, dh, 0, 1))
    if summed:
        finish_sum(hi_from)
        ready = stages[5]
        ready[...] = total_of(stages[1], n_hi).astype(ready.dtype)
        finish_sum = exchange(
            [ready] * n_col, stages[2], col, col_who, sum_local.at[2],
            sum_send, sum_recv, n_chan + n_hi - 2,
        )
    for h in range(2):
        for dh in range(1, n_hi):
            for dc in range(1, n_col):
                arrive(h, dh, dc, 0)
                send(h, dh, dc, sibling, slot_of(h, dh, dc, 1))
    if summed:
        finish_sum(col_from)
        ready = stages[6]
        ready[...] = total_of(stages[2], n_col)
        finish_sum = exchange(
            [ready] * 2, stages[3], core, core_who, sum_local.at[3],
            sum_send, sum_recv, n_chan + n_hi + n_col - 3,
        )
    for h in range(2):
        for dh in range(n_hi):
            for dc in range(n_col):
                arrive(h, dh, dc, 1)
    if summed:
        finish_sum([core, 1 - core])
        project_out[...] = total_of(stages[3], 2).astype(project_out.dtype)
    for finish in finish_extras:
        finish(chan_from)
    for copy in later:
        copy.wait_send()
    own.wait()
    for copy in sent:
        copy.wait_send()


def spread(cells, extras, project, collective_id):
    n_row, n_col, n_chan = (lax.axis_size(axis) for axis in ("row", "col", "chan"))
    n_hi = n_row // 2
    runs, rows, width = cells.shape
    tiles = n_hi * n_col
    shape = (runs * n_col + 2 * MARGIN_RUNS, rows * n_row + 2 * MARGIN_ROWS, width)
    copies = 2 * ((n_hi - 1) + (n_col - 1) * n_hi + tiles) + 2 * tiles
    vmem = pl.BlockSpec(memory_space=VMEM)
    dma = pltpu.SemaphoreType.DMA
    operands = [cells, *extras]
    outs = [jax.ShapeDtypeStruct(shape, cells.dtype)]
    outs += [jax.ShapeDtypeStruct((n_chan, *e.shape), e.dtype) for e in extras]
    scratch = [
        dma,
        dma((copies,)),
        dma((4 * tiles,)),
        dma((len(extras),)),
        dma((len(extras) * (n_chan - 1),)),
        dma((len(extras) * (n_chan - 1),)),
    ]
    if project is not None:
        slab = (project.shape[0], project.shape[1] // n_chan, project.shape[2])
        operands.append(project)
        outs.append(jax.ShapeDtypeStruct(slab, jnp.bfloat16))
        peers = n_chan + n_hi + n_col - 2
        scratch += [
            VMEM((n_chan, *slab), jnp.float32),
            VMEM((n_hi, *slab), jnp.bfloat16),
            VMEM((n_col, *slab), jnp.bfloat16),
            VMEM((2, *slab), jnp.float32),
            VMEM(slab, jnp.bfloat16),
            VMEM(slab, jnp.bfloat16),
            VMEM(slab, jnp.float32),
            dma((4,)),
            dma((peers,)),
            dma((peers,)),
        ]
    body = functools.partial(
        spread_kernel, n_row, n_col, n_chan, len(extras), project is not None
    )
    return pl.pallas_call(
        body,
        out_shape=tuple(outs),
        in_specs=[vmem] * len(operands),
        out_specs=(vmem,) * len(outs),
        scratch_shapes=scratch,
        compiler_params=pltpu.CompilerParams(
            collective_id=collective_id, has_side_effects=True, vmem_limit_bytes=LIMIT
        ),
        name="spread_tiles",
    )(*operands)


def tap_of(t):
    tap = jnp.maximum(t - 1, 0)
    branch = jnp.where(t == 0, 0, tap // 9 + 1)
    inner = tap % 9
    down = jnp.where(t == 0, 0, (inner // 3 - 1) * branch)
    across = jnp.where(t == 0, 0, (inner % 3 - 1) * branch)
    return branch, down, across


def forward_kernel(runs, rows, x_ref, wp_ref, w_ref, out_ref, total):
    t = pl.program_id(0)
    branch, down, across = tap_of(t)
    u0 = MARGIN_RUNS + runs * lax.axis_index("col") + across
    y0 = MARGIN_ROWS + rows * lax.axis_index("row") + down * (RATE_STEP * SLOT)
    width = x_ref.shape[-1]
    window = x_ref[pl.ds(u0, runs), pl.ds(pl.multiple_of(y0, 16), rows), :].reshape(
        runs * rows, width
    )
    weight = jnp.where(t == 0, wp_ref[...], w_ref[0])
    part = jnp.dot(window, weight, preferred_element_type=jnp.float32)
    fresh = jnp.logical_or(t == 0, lax.rem(t - 1, 9) == 0)

    @pl.when(fresh)
    def _():
        total[...] = part

    @pl.when(jnp.logical_not(fresh))
    def _():
        total[...] += part

    @pl.when(lax.rem(t, 9) == 0)
    def _():
        used = runs * rows
        out_ref[0, pl.ds(0, used), :] = total[...].astype(out_ref.dtype)
        if out_ref.shape[1] > used:
            out_ref[0, pl.ds(used, out_ref.shape[1] - used), :] = jnp.zeros(
                (out_ref.shape[1] - used, out_ref.shape[2]), out_ref.dtype
            )


def forward(spread_x, point_weight, taps, runs, rows, padded):
    width, out_count = point_weight.shape
    return pl.pallas_call(
        functools.partial(forward_kernel, runs, rows),
        grid=(28,),
        out_shape=jax.ShapeDtypeStruct((4, padded, out_count), jnp.bfloat16),
        in_specs=[
            pl.BlockSpec(memory_space=VMEM),
            pl.BlockSpec(memory_space=VMEM),
            pl.BlockSpec((1, width, out_count), lambda t: (jnp.maximum(t - 1, 0), 0, 0)),
        ],
        out_specs=pl.BlockSpec((1, padded, out_count), lambda t: ((t + 8) // 9, 0, 0)),
        scratch_shapes=[VMEM((runs * rows, out_count), jnp.float32)],
        compiler_params=pltpu.CompilerParams(
            dimension_semantics=("arbitrary",), vmem_limit_bytes=LIMIT
        ),
        name="forward_taps",
    )(spread_x, point_weight, taps)


def middle_kernel(
    n_chan, part_ref, gain_ref, shift_ref, pw_ref, pshift_ref, cot_ref,
    out_ref, project_ref, grad_ref, landed, own, send_sems, recv_sems, send2, recv2, local_sem,
):
    me = lax.axis_index("chan")
    size = cot_ref.shape[0]
    width = gain_ref.shape[1]
    peers = [lax.rem(me + d, n_chan) for d in range(n_chan)]
    froms = [lax.rem(me - d + n_chan, n_chan) for d in range(n_chan)]
    barrier = pltpu.get_barrier_semaphore()
    for d in range(1, n_chan):
        pl.semaphore_signal(barrier, inc=1, device_id={"chan": peers[d]}, device_id_type=MESH)
    pl.semaphore_wait(barrier, n_chan - 1)
    copies = []
    for d in range(1, n_chan):
        copy = pltpu.make_async_remote_copy(
            src_ref=part_ref.at[:, pl.ds(pl.multiple_of(peers[d] * size, 16), size), :],
            dst_ref=landed.at[d - 1],
            send_sem=send_sems.at[d - 1],
            recv_sem=recv_sems.at[d - 1],
            device_id={"chan": peers[d]},
            device_id_type=MESH,
        )
        copy.start()
        copies.append(copy)
    for copy in copies:
        copy.wait_recv()
    acts = []
    mixed = jnp.zeros((size, width), jnp.float32)
    hiddens = []
    mine = pl.ds(pl.multiple_of(me * size, 16), size)
    for b in range(4):
        pre = part_ref[b, mine, :].astype(jnp.float32)
        for d in range(n_chan - 1):
            pre = pre + landed[d, b].astype(jnp.float32)
        act = pre * gain_ref[b][None, :] + shift_ref[b][None, :]
        hidden = (act * jax.nn.sigmoid(act)).astype(jnp.bfloat16)
        acts.append(act)
        hiddens.append(hidden)
        mixed = mixed + jnp.dot(hidden, pw_ref[b], preferred_element_type=jnp.float32)
    mixed_act = mixed + pshift_ref[...]
    logistic = jax.nn.sigmoid(mixed_act)
    out_ref[...] = (mixed_act * logistic).astype(jnp.bfloat16)
    mixed_grad = (
        cot_ref[...].astype(jnp.float32) * (logistic * (1.0 + mixed_act * (1.0 - logistic)))
    ).astype(jnp.bfloat16)
    for b in range(4):
        hidden_grad = lax.dot_general(
            mixed_grad, pw_ref[b], (((1,), (1,)), ((), ())), preferred_element_type=jnp.float32
        )
        own[:, b * width : (b + 1) * width] = (
            hidden_grad * silu_slope(acts[b]) * gain_ref[b][None, :]
        ).astype(jnp.bfloat16)
    place = grad_ref.at[mine, :]
    local = pltpu.make_async_copy(own, place, local_sem)
    local.start()
    grads = []
    for d in range(1, n_chan):
        copy = pltpu.make_async_remote_copy(
            src_ref=own,
            dst_ref=place,
            send_sem=send2.at[d - 1],
            recv_sem=recv2.at[d - 1],
            device_id={"chan": peers[d]},
            device_id_type=MESH,
        )
        copy.start()
        grads.append(copy)
    for b in range(4):
        project_ref[b] = lax.dot_general(
            hiddens[b], mixed_grad, (((0,), (0,)), ((), ())), preferred_element_type=jnp.float32
        )
    local.wait()
    for d in range(1, n_chan):
        there = grad_ref.at[pl.ds(pl.multiple_of(froms[d] * size, 16), size), :]
        pltpu.make_async_remote_copy(
            src_ref=own,
            dst_ref=there,
            send_sem=send2.at[d - 1],
            recv_sem=recv2.at[d - 1],
            device_id={"chan": peers[d]},
            device_id_type=MESH,
        ).wait_recv()
    for copy in copies + grads:
        copy.wait_send()


def middle(part, gain, shift, pw, pshift, cot):
    n_chan = lax.axis_size("chan")
    size, width = cot.shape
    vmem = pl.BlockSpec(memory_space=VMEM)
    dma = pltpu.SemaphoreType.DMA((n_chan - 1,))
    return pl.pallas_call(
        functools.partial(middle_kernel, n_chan),
        out_shape=(
            jax.ShapeDtypeStruct((size, width), jnp.bfloat16),
            jax.ShapeDtypeStruct((4, width, width), jnp.float32),
            jax.ShapeDtypeStruct((size * n_chan, 4 * width), jnp.bfloat16),
        ),
        in_specs=[vmem] * 6,
        out_specs=(vmem,) * 3,
        scratch_shapes=[
            VMEM((n_chan - 1, 4, size, width), jnp.bfloat16),
            VMEM((size, 4 * width), jnp.bfloat16),
            dma, dma, dma, dma,
            pltpu.SemaphoreType.DMA,
        ],
        compiler_params=pltpu.CompilerParams(
            collective_id=2, has_side_effects=True, vmem_limit_bytes=LIMIT
        ),
        name="middle",
    )(part, gain, shift, pw, pshift, cot)


def backward_kernel(
    runs, rows, xt_ref, b_ref, wp_ref, w_ref, in_ref, dil_ref,
    total, grad, held, keep_sems, send_sems, recv_sems,
):
    t = pl.program_id(0)
    branch, down, across = tap_of(t)
    pairs, half, depth = xt_ref.shape
    out_count = b_ref.shape[-1]
    full_rows = b_ref.shape[1] - 2 * MARGIN_ROWS
    y_off = pl.multiple_of(MARGIN_ROWS - down * (RATE_STEP * SLOT), 16)
    row = lax.axis_index("row")
    core = row % 2
    sibling = {"row": row - core + 1 - core}
    mine = pl.ds(pl.multiple_of(core * half, 16), half)
    other = pl.ds(pl.multiple_of((1 - core) * half, 16), half)

    @pl.when(t == 0)
    def _():
        barrier = pltpu.get_barrier_semaphore()
        pl.semaphore_signal(barrier, inc=1, device_id=sibling, device_id_type=MESH)
        pl.semaphore_wait(barrier, 1)

    def moves(step, slot):
        keep = pltpu.make_async_copy(held.at[slot], dil_ref.at[step, mine, :], keep_sems.at[slot])
        give = pltpu.make_async_remote_copy(
            src_ref=held.at[slot],
            dst_ref=dil_ref.at[step, mine, :],
            send_sem=send_sems.at[slot],
            recv_sem=recv_sems.at[step],
            device_id=sibling,
            device_id_type=MESH,
        )
        return keep, give

    slot = lax.rem(t, 2)
    for g in range(pairs):
        cells = b_ref[pl.ds(MARGIN_RUNS - across + 2 * g, 2), pl.ds(y_off, full_rows), :]
        part = jnp.dot(
            xt_ref[g], cells.reshape(depth, out_count), preferred_element_type=jnp.float32
        )
        if g == 0:
            grad[...] = part
        else:
            grad[...] += part

    @pl.when(t >= 2)
    def _():
        keep, give = moves(t - 2, slot)
        keep.wait()
        give.wait_send()

    held[slot] = grad[...].astype(jnp.bfloat16)
    keep, give = moves(t, slot)
    keep.start()
    give.start()

    u0 = MARGIN_RUNS + runs * lax.axis_index("col") - across
    y0 = MARGIN_ROWS + rows * row - down * (RATE_STEP * SLOT)
    window = b_ref[pl.ds(u0, runs), pl.ds(pl.multiple_of(y0, 16), rows), :].reshape(
        runs * rows, out_count
    )
    weight = jnp.where(t == 0, wp_ref[...], w_ref[0])
    part = lax.dot_general(
        window, weight, (((1,), (1,)), ((), ())), preferred_element_type=jnp.float32
    )

    @pl.when(t == 0)
    def _():
        total[...] = part

    @pl.when(t > 0)
    def _():
        total[...] += part

    @pl.when(t == 27)
    def _():
        in_ref[...] = total[...].astype(jnp.bfloat16)
        for step in (26, 27):
            keep, give = moves(step, step % 2)
            keep.wait()
            give.wait_send()

        def landed(step, _):
            there = dil_ref.at[step, other, :]
            pltpu.make_async_remote_copy(
                src_ref=there,
                dst_ref=there,
                send_sem=send_sems.at[0],
                recv_sem=recv_sems.at[step],
                device_id=sibling,
                device_id_type=MESH,
            ).wait_recv()
            return 0

        lax.fori_loop(0, 28, landed, 0)


def backward(xt, spread_b, point_weight, taps, runs, rows):
    width, out_count = point_weight.shape
    total_runs, total_rows, _ = spread_b.shape
    half = width // 2
    tap_index = lambda t: (jnp.maximum(t - 1, 0), 0, 0)
    return pl.pallas_call(
        functools.partial(backward_kernel, runs, rows),
        grid=(28,),
        out_shape=(
            jax.ShapeDtypeStruct((runs * rows, width), jnp.bfloat16),
            jax.ShapeDtypeStruct((28, width, out_count), jnp.bfloat16),
        ),
        in_specs=[
            pl.BlockSpec(memory_space=VMEM),
            pl.BlockSpec((total_runs, total_rows, out_count), lambda t: (0, 0, (t + 8) // 9)),
            pl.BlockSpec(memory_space=VMEM),
            pl.BlockSpec((1, width, out_count), tap_index),
        ],
        out_specs=(
            pl.BlockSpec((runs * rows, width), lambda t: (0, 0)),
            pl.BlockSpec(memory_space=pl.ANY),
        ),
        scratch_shapes=[
            VMEM((runs * rows, width), jnp.float32),
            VMEM((half, out_count), jnp.float32),
            VMEM((2, half, out_count), jnp.bfloat16),
            pltpu.SemaphoreType.DMA((2,)),
            pltpu.SemaphoreType.DMA((2,)),
            pltpu.SemaphoreType.DMA((28,)),
        ],
        compiler_params=pltpu.CompilerParams(
            dimension_semantics=("arbitrary",),
            vmem_limit_bytes=LIMIT,
            collective_id=3,
            has_side_effects=True,
        ),
        name="backward_taps",
    )(xt, spread_b, point_weight, taps)


def per_device(
    features,
    dilated_weight,
    point_weight,
    branch_gain,
    branch_shift,
    project_weight,
    project_shift,
    cotangent,
):
    local_in, tile_h, tile_w = features.shape
    out_count = point_weight.shape[1]
    local_out = branch_gain.shape[0]
    n_chan = lax.axis_size("chan")
    me = lax.axis_index("chan")
    runs, rows = tile_w // RATE_STEP, tile_h * SLOT
    used = runs * rows
    size = (-(-used // n_chan) + 15) // 16 * 16
    padded = size * n_chan
    taps = dilated_weight.reshape(27, local_in, out_count)

    vectors = jnp.concatenate([branch_gain, branch_shift, project_shift[:, None]], axis=1)
    cot = to_runs(cotangent).reshape(used, local_out)
    cot = jnp.pad(cot, ((0, padded - used), (0, 0)))
    spread_x, vectors, pw, cot = spread(
        to_runs(features), [vectors, project_weight.transpose(1, 0, 2), cot], None, 0
    )
    vectors = vectors.transpose(2, 0, 1).reshape(9, out_count)
    gain, shift, pshift = vectors[:4], vectors[4:8], vectors[8:9]
    pw = pw.transpose(1, 0, 2, 3).reshape(4, out_count, out_count)
    cot = lax.dynamic_slice_in_dim(cot, me * size, size, axis=1)
    cot = cot.transpose(1, 0, 2).reshape(size, out_count)

    part = forward(spread_x, point_weight, taps, runs, rows, padded)
    mixed_out, project, grads = middle(part, gain, shift, pw, pshift, cot)
    spread_b, mixed_out, project = spread(
        grads[:used].reshape(runs, rows, 4 * out_count), [mixed_out], project, 1
    )

    total_runs, total_rows, _ = spread_x.shape
    inner = spread_x[MARGIN_RUNS:-MARGIN_RUNS, MARGIN_ROWS:-MARGIN_ROWS]
    pairs = inner.shape[0] // 2
    half = local_in // 2
    inner = lax.dynamic_slice_in_dim(inner, lax.axis_index("row") % 2 * half, half, axis=2)
    xt = inner.reshape(pairs, 2 * inner.shape[1], half).transpose(0, 2, 1)
    input_grad, weight_grads = backward(
        xt, spread_b, point_weight, taps, runs, rows
    )

    mixed_out = lax.dynamic_slice_in_dim(mixed_out, me * local_out, local_out, axis=2)
    mixed_out = from_runs(mixed_out.reshape(padded, local_out)[:used], tile_h, tile_w)
    return (
        mixed_out,
        from_runs(input_grad, tile_h, tile_w),
        weight_grads[1:].reshape(dilated_weight.shape),
        weight_grads[0],
        project.transpose(1, 0, 2),
    )


def solution(mesh):
    placed = (
        P("chan", "row", "col"),
        P(None, None, None, "chan", None),
        P("chan", None),
        P("chan", None),
        P("chan", None),
        P("chan", None, None),
        P("chan"),
        P("chan", "row", "col"),
    )
    return jax.shard_map(
        per_device,
        mesh=mesh,
        in_specs=placed,
        out_specs=(
            P("chan", "row", "col"),
            P("chan", "row", "col"),
            P(None, None, None, "chan", None),
            P("chan", None),
            P("chan", None, None),
        ),
        check_vma=False,
    )
```

```python
import functools

import jax
import jax.numpy as jnp
from jax import lax
from jax.experimental import pallas as pl
from jax.experimental.pallas import tpu as pltpu
from jax.sharding import PartitionSpec as P

RATE_STEP = 6
SLOT = 8
MARGIN_RUNS = 3
MARGIN_ROWS = 3 * RATE_STEP * SLOT
MESH = pl.DeviceIdType.MESH
VMEM = pltpu.VMEM
LIMIT = 67_000_000


def silu_slope(values):
    logistic = jax.nn.sigmoid(values)
    return logistic * (1.0 + values * (1.0 - logistic))


def to_runs(cells):
    count, tile_h, tile_w = cells.shape
    runs = tile_w // RATE_STEP
    cells = cells.reshape(count, tile_h, runs, RATE_STEP)
    cells = jnp.pad(cells, ((0, 0), (0, 0), (0, 0), (0, SLOT - RATE_STEP)))
    return cells.transpose(2, 1, 3, 0).reshape(runs, tile_h * SLOT, count)


def from_runs(cells, tile_h, tile_w):
    runs = tile_w // RATE_STEP
    count = cells.shape[-1]
    cells = cells.reshape(runs, tile_h, SLOT, count)[:, :, :RATE_STEP]
    return cells.transpose(3, 1, 0, 2).reshape(count, tile_h, tile_w)


def spread_kernel(n_row, n_col, n_chan, n_extra, summed, *refs):
    x_ref, extras, refs = refs[0], refs[1 : 1 + n_extra], refs[1 + n_extra :]
    if summed:
        project_ref, refs = refs[0], refs[1:]
    out_ref, gathered, refs = refs[0], refs[1 : 1 + n_extra], refs[1 + n_extra :]
    if summed:
        project_out, refs = refs[0], refs[1:]
    local_sem, send_sems, recv_sems, extra_local, extra_send, extra_recv = refs[:6]
    if summed:
        stages, sum_local, sum_send, sum_recv = refs[6:13], refs[13], refs[14], refs[15]
    n_hi = n_row // 2
    chan = lax.axis_index("chan")
    chan_peer = [lax.rem(chan + d, n_chan) for d in range(n_chan)]
    chan_from = [lax.rem(chan - d + n_chan, n_chan) for d in range(n_chan)]
    row = lax.axis_index("row")
    col = lax.axis_index("col")
    hi, core = row // 2, row % 2
    runs, rows, _ = x_ref.shape
    first = (rows // 2 + 15) // 16 * 16
    starts, sizes = (0, first), (first, rows - first)

    hi_peer = [lax.rem(hi + d, n_hi) for d in range(n_hi)]
    hi_from = [lax.rem(hi - d + n_hi, n_hi) for d in range(n_hi)]
    col_peer = [lax.rem(col + d, n_col) for d in range(n_col)]
    col_from = [lax.rem(col - d + n_col, n_col) for d in range(n_col)]
    sibling = {"row": hi * 2 + 1 - core}
    partners = [sibling]
    partners += [{"row": hi_peer[d] * 2 + core} for d in range(1, n_hi)]
    partners += [{"col": col_peer[d]} for d in range(1, n_col)]
    partners += [{"chan": chan_peer[d]} for d in range(1, n_chan)]

    barrier = pltpu.get_barrier_semaphore()
    for who in partners:
        pl.semaphore_signal(barrier, inc=1, device_id=who, device_id_type=MESH)

    dtype = out_ref.dtype
    total_runs, total_rows, width = out_ref.shape
    edge = jnp.zeros((MARGIN_ROWS, width), dtype)

    def clear_run(u, _):
        for at in (u, total_runs - MARGIN_RUNS + u):
            for y in range(0, total_rows, MARGIN_ROWS):
                out_ref[at, pl.ds(y, MARGIN_ROWS), :] = edge
        return 0

    def clear_ends(u, _):
        out_ref[u, pl.ds(0, MARGIN_ROWS), :] = edge
        out_ref[u, pl.ds(total_rows - MARGIN_ROWS, MARGIN_ROWS), :] = edge
        return 0

    pl.semaphore_wait(barrier, len(partners))

    def place(h, hi_, core_, col_):
        return out_ref.at[
            pl.ds(MARGIN_RUNS + runs * col_, runs),
            pl.ds(pl.multiple_of(MARGIN_ROWS + (hi_ * 2 + core_) * rows + starts[h], 16), sizes[h]),
            :,
        ]

    sent = []

    def send(h, dh, dc, who, slot):
        if dh == 0 and dc == 0:
            src = x_ref.at[:, pl.ds(starts[h], sizes[h]), :]
        else:
            src = place(h, hi_from[dh], core, col_from[dc])
        copy = pltpu.make_async_remote_copy(
            src_ref=src,
            dst_ref=place(h, hi_from[dh], core, col_from[dc]),
            send_sem=send_sems.at[len(sent)],
            recv_sem=recv_sems.at[slot],
            device_id=who,
            device_id_type=MESH,
        )
        copy.start()
        sent.append(copy)

    def slot_of(h, dh, dc, side):
        return ((h * n_hi + dh) * n_col + dc) * 2 + side

    def arrive(h, dh, dc, side):
        core_ = core if side == 0 else 1 - core
        here = place(h, hi_from[dh], core_, col_from[dc])
        pltpu.make_async_remote_copy(
            src_ref=here,
            dst_ref=here,
            send_sem=send_sems.at[0],
            recv_sem=recv_sems.at[slot_of(h, dh, dc, side)],
            device_id=sibling,
            device_id_type=MESH,
        ).wait_recv()

    later = []

    def exchange(sources, landing, at, who, local, sends, recvs, base):
        keep = pltpu.make_async_copy(sources[0], landing.at[at], local)
        keep.start()
        for d in range(1, len(sources)):
            copy = pltpu.make_async_remote_copy(
                src_ref=sources[d],
                dst_ref=landing.at[at],
                send_sem=sends.at[base + d - 1],
                recv_sem=recvs.at[base + d - 1],
                device_id=who[d],
                device_id_type=MESH,
            )
            copy.start()
            later.append(copy)

        def finish(froms):
            keep.wait()
            for d in range(1, len(sources)):
                pltpu.make_async_remote_copy(
                    src_ref=landing.at[froms[d]],
                    dst_ref=landing.at[froms[d]],
                    send_sem=sends.at[base + d - 1],
                    recv_sem=recvs.at[base + d - 1],
                    device_id=who[d],
                    device_id_type=MESH,
                ).wait_recv()

        return finish

    chan_who = [{"chan": chan_peer[d]} for d in range(n_chan)]
    for d in range(1, n_hi):
        send(0, 0, 0, {"row": hi_peer[d] * 2 + core}, slot_of(0, d, 0, 0))
    for d in range(1, n_col):
        send(1, 0, 0, {"col": col_peer[d]}, slot_of(1, 0, d, 0))
    if summed:
        slab = project_ref.shape[1] // n_chan
        slabs = [
            project_ref.at[:, pl.ds(pl.multiple_of(chan_peer[d] * slab, 8), slab), :]
            for d in range(n_chan)
        ]
        finish_sum = exchange(
            slabs, stages[0], chan, chan_who, sum_local.at[0], sum_send, sum_recv, 0
        )
        hi_who = [{"row": hi_peer[d] * 2 + core} for d in range(n_hi)]
        col_who = [{"col": col_peer[d]} for d in range(n_col)]
        core_who = [sibling, sibling]

    def total_of(stage, count):
        value = stage[0].astype(jnp.float32)
        for i in range(1, count):
            value = value + stage[i].astype(jnp.float32)
        return value

    finish_extras = [
        exchange(
            [extras[i]] * n_chan, gathered[i], chan, chan_who,
            extra_local.at[i], extra_send, extra_recv, i * (n_chan - 1),
        )
        for i in range(n_extra)
    ]
    for d in range(1, n_col):
        send(0, 0, 0, {"col": col_peer[d]}, slot_of(0, 0, d, 0))
    for d in range(1, n_hi):
        send(1, 0, 0, {"row": hi_peer[d] * 2 + core}, slot_of(1, d, 0, 0))
    for h in range(2):
        send(h, 0, 0, sibling, slot_of(h, 0, 0, 1))
    own = pltpu.make_async_copy(
        x_ref,
        out_ref.at[
            pl.ds(MARGIN_RUNS + runs * col, runs),
            pl.ds(pl.multiple_of(MARGIN_ROWS + row * rows, 16), rows),
            :,
        ],
        local_sem,
    )
    own.start()
    lax.fori_loop(0, MARGIN_RUNS, clear_run, 0)
    lax.fori_loop(MARGIN_RUNS, total_runs - MARGIN_RUNS, clear_ends, 0)

    for dh in range(1, n_hi):
        arrive(0, dh, 0, 0)
        for d in range(1, n_col):
            send(0, dh, 0, {"col": col_peer[d]}, slot_of(0, dh, d, 0))
        send(0, dh, 0, sibling, slot_of(0, dh, 0, 1))
    for dc in range(1, n_col):
        arrive(1, 0, dc, 0)
        for d in range(1, n_hi):
            send(1, 0, dc, {"row": hi_peer[d] * 2 + core}, slot_of(1, d, dc, 0))
        send(1, 0, dc, sibling, slot_of(1, 0, dc, 1))
    if summed:
        finish_sum(chan_from)
        ready = stages[4]
        ready[...] = total_of(stages[0], n_chan).astype(ready.dtype)
        finish_sum = exchange(
            [ready] * n_hi, stages[1], hi, hi_who, sum_local.at[1], sum_send, sum_recv, n_chan - 1
        )
    for dc in range(1, n_col):
        arrive(0, 0, dc, 0)
        send(0, 0, dc, sibling, slot_of(0, 0, dc, 1))
    for dh in range(1, n_hi):
        arrive(1, dh, 0, 0)
        send(1, dh, 0, sibling, slot_of(1, dh, 0, 1))
    if summed:
        finish_sum(hi_from)
        ready = stages[5]
        ready[...] = total_of(stages[1], n_hi).astype(ready.dtype)
        finish_sum = exchange(
            [ready] * n_col, stages[2], col, col_who, sum_local.at[2],
            sum_send, sum_recv, n_chan + n_hi - 2,
        )
    for h in range(2):
        for dh in range(1, n_hi):
            for dc in range(1, n_col):
                arrive(h, dh, dc, 0)
                send(h, dh, dc, sibling, slot_of(h, dh, dc, 1))
    if summed:
        finish_sum(col_from)
        ready = stages[6]
        ready[...] = total_of(stages[2], n_col)
        finish_sum = exchange(
            [ready] * 2, stages[3], core, core_who, sum_local.at[3],
            sum_send, sum_recv, n_chan + n_hi + n_col - 3,
        )
    for h in range(2):
        for dh in range(n_hi):
            for dc in range(n_col):
                arrive(h, dh, dc, 1)
    if summed:
        finish_sum([core, 1 - core])
        project_out[...] = total_of(stages[3], 2).astype(project_out.dtype)
    for finish in finish_extras:
        finish(chan_from)
    for copy in later:
        copy.wait_send()
    own.wait()
    for copy in sent:
        copy.wait_send()


def spread(cells, extras, project, collective_id):
    n_row, n_col, n_chan = (lax.axis_size(axis) for axis in ("row", "col", "chan"))
    n_hi = n_row // 2
    runs, rows, width = cells.shape
    tiles = n_hi * n_col
    shape = (runs * n_col + 2 * MARGIN_RUNS, rows * n_row + 2 * MARGIN_ROWS, width)
    copies = 2 * ((n_hi - 1) + (n_col - 1) * n_hi + tiles) + 2 * tiles
    vmem = pl.BlockSpec(memory_space=VMEM)
    dma = pltpu.SemaphoreType.DMA
    operands = [cells, *extras]
    outs = [jax.ShapeDtypeStruct(shape, cells.dtype)]
    outs += [jax.ShapeDtypeStruct((n_chan, *e.shape), e.dtype) for e in extras]
    scratch = [
        dma,
        dma((copies,)),
        dma((4 * tiles,)),
        dma((len(extras),)),
        dma((len(extras) * (n_chan - 1),)),
        dma((len(extras) * (n_chan - 1),)),
    ]
    if project is not None:
        slab = (project.shape[0], project.shape[1] // n_chan, project.shape[2])
        operands.append(project)
        outs.append(jax.ShapeDtypeStruct(slab, jnp.bfloat16))
        peers = n_chan + n_hi + n_col - 2
        scratch += [
            VMEM((n_chan, *slab), jnp.float32),
            VMEM((n_hi, *slab), jnp.bfloat16),
            VMEM((n_col, *slab), jnp.bfloat16),
            VMEM((2, *slab), jnp.float32),
            VMEM(slab, jnp.bfloat16),
            VMEM(slab, jnp.bfloat16),
            VMEM(slab, jnp.float32),
            dma((4,)),
            dma((peers,)),
            dma((peers,)),
        ]
    body = functools.partial(
        spread_kernel, n_row, n_col, n_chan, len(extras), project is not None
    )
    return pl.pallas_call(
        body,
        out_shape=tuple(outs),
        in_specs=[vmem] * len(operands),
        out_specs=(vmem,) * len(outs),
        scratch_shapes=scratch,
        compiler_params=pltpu.CompilerParams(
            collective_id=collective_id, has_side_effects=True, vmem_limit_bytes=LIMIT
        ),
        name="spread_tiles",
    )(*operands)


def tap_of(t):
    tap = jnp.maximum(t - 1, 0)
    branch = jnp.where(t == 0, 0, tap // 9 + 1)
    inner = tap % 9
    down = jnp.where(t == 0, 0, (inner // 3 - 1) * branch)
    across = jnp.where(t == 0, 0, (inner % 3 - 1) * branch)
    return branch, down, across


def forward_kernel(
    runs, rows, n_chan, x_ref, wp_ref, w_ref, out_ref,
    total, held, landed, send_sems, recv_sems, local_sems,
):
    t = pl.program_id(0)
    me = lax.axis_index("chan")
    size = out_ref.shape[1]
    peers = [lax.rem(me + d, n_chan) for d in range(n_chan)]

    @pl.when(t == 0)
    def _():
        barrier = pltpu.get_barrier_semaphore()
        for d in range(1, n_chan):
            pl.semaphore_signal(
                barrier, inc=1, device_id={"chan": peers[d]}, device_id_type=MESH
            )
        pl.semaphore_wait(barrier, n_chan - 1)

    def share(b, d):
        return held.at[b, pl.ds(pl.multiple_of(peers[d] * size, 16), size), :]

    def keep(b):
        return pltpu.make_async_copy(share(b, 0), landed.at[0, b], local_sems.at[b])

    def give(b, d):
        return pltpu.make_async_remote_copy(
            src_ref=share(b, d),
            dst_ref=landed.at[d, b],
            send_sem=send_sems.at[b, d],
            recv_sem=recv_sems.at[b, d],
            device_id={"chan": peers[d]},
            device_id_type=MESH,
        )

    branch, down, across = tap_of(t)
    u0 = MARGIN_RUNS + runs * lax.axis_index("col") + across
    y0 = MARGIN_ROWS + rows * lax.axis_index("row") + down * (RATE_STEP * SLOT)
    width = x_ref.shape[-1]
    window = x_ref[pl.ds(u0, runs), pl.ds(pl.multiple_of(y0, 16), rows), :].reshape(
        runs * rows, width
    )
    weight = jnp.where(t == 0, wp_ref[...], w_ref[0])
    part = jnp.dot(window, weight, preferred_element_type=jnp.float32)
    fresh = jnp.logical_or(t == 0, lax.rem(t - 1, 9) == 0)

    @pl.when(fresh)
    def _():
        total[...] = part

    @pl.when(jnp.logical_not(fresh))
    def _():
        total[...] += part

    used = runs * rows
    for b in range(4):

        @pl.when(t == 9 * b)
        def _():
            held[b, pl.ds(0, used), :] = total[...].astype(held.dtype)
            if held.shape[1] > used:
                held[b, pl.ds(used, held.shape[1] - used), :] = jnp.zeros(
                    (held.shape[1] - used, held.shape[2]), held.dtype
                )
            keep(b).start()
            for d in range(1, n_chan):
                give(b, d).start()

    @pl.when(t == 27)
    def _():
        for b in range(4):
            keep(b).wait()
            for d in range(1, n_chan):
                give(b, d).wait()
            pre = landed[0, b].astype(jnp.float32)
            for d in range(1, n_chan):
                pre = pre + landed[d, b].astype(jnp.float32)
            out_ref[b] = pre


def forward(spread_x, point_weight, taps, runs, rows, size):
    width, out_count = point_weight.shape
    n_chan = lax.axis_size("chan")
    return pl.pallas_call(
        functools.partial(forward_kernel, runs, rows, n_chan),
        grid=(28,),
        out_shape=jax.ShapeDtypeStruct((4, size, out_count), jnp.float32),
        in_specs=[
            pl.BlockSpec(memory_space=VMEM),
            pl.BlockSpec(memory_space=VMEM),
            pl.BlockSpec((1, width, out_count), lambda t: (jnp.maximum(t - 1, 0), 0, 0)),
        ],
        out_specs=pl.BlockSpec((4, size, out_count), lambda t: (0, 0, 0)),
        scratch_shapes=[
            VMEM((runs * rows, out_count), jnp.float32),
            VMEM((4, size * n_chan, out_count), jnp.bfloat16),
            VMEM((n_chan, 4, size, out_count), jnp.bfloat16),
            pltpu.SemaphoreType.DMA((4, n_chan)),
            pltpu.SemaphoreType.DMA((4, n_chan)),
            pltpu.SemaphoreType.DMA((4,)),
        ],
        compiler_params=pltpu.CompilerParams(
            dimension_semantics=("arbitrary",),
            vmem_limit_bytes=LIMIT,
            collective_id=4,
            has_side_effects=True,
        ),
        name="forward_taps",
    )(spread_x, point_weight, taps)


def middle_kernel(
    n_chan, part_ref, gain_ref, shift_ref, pw_ref, pshift_ref, cot_ref,
    out_ref, project_ref, grad_ref, own, send2, recv2, local_sem,
):
    me = lax.axis_index("chan")
    size = cot_ref.shape[0]
    width = gain_ref.shape[1]
    peers = [lax.rem(me + d, n_chan) for d in range(n_chan)]
    froms = [lax.rem(me - d + n_chan, n_chan) for d in range(n_chan)]
    barrier = pltpu.get_barrier_semaphore()
    for d in range(1, n_chan):
        pl.semaphore_signal(barrier, inc=1, device_id={"chan": peers[d]}, device_id_type=MESH)
    pl.semaphore_wait(barrier, n_chan - 1)
    acts = []
    mixed = jnp.zeros((size, width), jnp.float32)
    hiddens = []
    mine = pl.ds(pl.multiple_of(me * size, 16), size)
    for b in range(4):
        act = part_ref[b] * gain_ref[b][None, :] + shift_ref[b][None, :]
        hidden = (act * jax.nn.sigmoid(act)).astype(jnp.bfloat16)
        acts.append(act)
        hiddens.append(hidden)
        mixed = mixed + jnp.dot(hidden, pw_ref[b], preferred_element_type=jnp.float32)
    mixed_act = mixed + pshift_ref[...]
    logistic = jax.nn.sigmoid(mixed_act)
    out_ref[...] = (mixed_act * logistic).astype(jnp.bfloat16)
    mixed_grad = (
        cot_ref[...].astype(jnp.float32) * (logistic * (1.0 + mixed_act * (1.0 - logistic)))
    ).astype(jnp.bfloat16)
    for b in range(4):
        hidden_grad = lax.dot_general(
            mixed_grad, pw_ref[b], (((1,), (1,)), ((), ())), preferred_element_type=jnp.float32
        )
        own[:, b * width : (b + 1) * width] = (
            hidden_grad * silu_slope(acts[b]) * gain_ref[b][None, :]
        ).astype(jnp.bfloat16)
    place = grad_ref.at[mine, :]
    local = pltpu.make_async_copy(own, place, local_sem)
    local.start()
    grads = []
    for d in range(1, n_chan):
        copy = pltpu.make_async_remote_copy(
            src_ref=own,
            dst_ref=place,
            send_sem=send2.at[d - 1],
            recv_sem=recv2.at[d - 1],
            device_id={"chan": peers[d]},
            device_id_type=MESH,
        )
        copy.start()
        grads.append(copy)
    for b in range(4):
        project_ref[b] = lax.dot_general(
            hiddens[b], mixed_grad, (((0,), (0,)), ((), ())), preferred_element_type=jnp.float32
        )
    local.wait()
    for d in range(1, n_chan):
        there = grad_ref.at[pl.ds(pl.multiple_of(froms[d] * size, 16), size), :]
        pltpu.make_async_remote_copy(
            src_ref=own,
            dst_ref=there,
            send_sem=send2.at[d - 1],
            recv_sem=recv2.at[d - 1],
            device_id={"chan": peers[d]},
            device_id_type=MESH,
        ).wait_recv()
    for copy in grads:
        copy.wait_send()


def middle(part, gain, shift, pw, pshift, cot):
    n_chan = lax.axis_size("chan")
    size, width = cot.shape
    vmem = pl.BlockSpec(memory_space=VMEM)
    dma = pltpu.SemaphoreType.DMA((n_chan - 1,))
    return pl.pallas_call(
        functools.partial(middle_kernel, n_chan),
        out_shape=(
            jax.ShapeDtypeStruct((size, width), jnp.bfloat16),
            jax.ShapeDtypeStruct((4, width, width), jnp.float32),
            jax.ShapeDtypeStruct((size * n_chan, 4 * width), jnp.bfloat16),
        ),
        in_specs=[vmem] * 6,
        out_specs=(vmem,) * 3,
        scratch_shapes=[
            VMEM((size, 4 * width), jnp.bfloat16),
            dma, dma,
            pltpu.SemaphoreType.DMA,
        ],
        compiler_params=pltpu.CompilerParams(
            collective_id=2, has_side_effects=True, vmem_limit_bytes=LIMIT
        ),
        name="middle",
    )(part, gain, shift, pw, pshift, cot)


def backward_kernel(
    runs, rows, xt_ref, b_ref, wp_ref, w_ref, in_ref, dil_ref,
    total, grad, held, keep_sems, send_sems, recv_sems,
):
    t = pl.program_id(0)
    branch, down, across = tap_of(t)
    pairs, half, depth = xt_ref.shape
    out_count = b_ref.shape[-1]
    full_rows = b_ref.shape[1] - 2 * MARGIN_ROWS
    y_off = pl.multiple_of(MARGIN_ROWS - down * (RATE_STEP * SLOT), 16)
    row = lax.axis_index("row")
    core = row % 2
    sibling = {"row": row - core + 1 - core}
    mine = pl.ds(pl.multiple_of(core * half, 16), half)
    other = pl.ds(pl.multiple_of((1 - core) * half, 16), half)

    @pl.when(t == 0)
    def _():
        barrier = pltpu.get_barrier_semaphore()
        pl.semaphore_signal(barrier, inc=1, device_id=sibling, device_id_type=MESH)
        pl.semaphore_wait(barrier, 1)

    def moves(step, slot):
        keep = pltpu.make_async_copy(held.at[slot], dil_ref.at[step, mine, :], keep_sems.at[slot])
        give = pltpu.make_async_remote_copy(
            src_ref=held.at[slot],
            dst_ref=dil_ref.at[step, mine, :],
            send_sem=send_sems.at[slot],
            recv_sem=recv_sems.at[step],
            device_id=sibling,
            device_id_type=MESH,
        )
        return keep, give

    slot = lax.rem(t, 2)
    for g in range(pairs):
        cells = b_ref[pl.ds(MARGIN_RUNS - across + 2 * g, 2), pl.ds(y_off, full_rows), :]
        part = jnp.dot(
            xt_ref[g], cells.reshape(depth, out_count), preferred_element_type=jnp.float32
        )
        if g == 0:
            grad[...] = part
        else:
            grad[...] += part

    @pl.when(t >= 2)
    def _():
        keep, give = moves(t - 2, slot)
        keep.wait()
        give.wait_send()

    held[slot] = grad[...].astype(jnp.bfloat16)
    keep, give = moves(t, slot)
    keep.start()
    give.start()

    u0 = MARGIN_RUNS + runs * lax.axis_index("col") - across
    y0 = MARGIN_ROWS + rows * row - down * (RATE_STEP * SLOT)
    window = b_ref[pl.ds(u0, runs), pl.ds(pl.multiple_of(y0, 16), rows), :].reshape(
        runs * rows, out_count
    )
    weight = jnp.where(t == 0, wp_ref[...], w_ref[0])
    part = lax.dot_general(
        window, weight, (((1,), (1,)), ((), ())), preferred_element_type=jnp.float32
    )

    @pl.when(t == 0)
    def _():
        total[...] = part

    @pl.when(t > 0)
    def _():
        total[...] += part

    @pl.when(t == 27)
    def _():
        in_ref[...] = total[...].astype(jnp.bfloat16)
        for step in (26, 27):
            keep, give = moves(step, step % 2)
            keep.wait()
            give.wait_send()

        def landed(step, _):
            there = dil_ref.at[step, other, :]
            pltpu.make_async_remote_copy(
                src_ref=there,
                dst_ref=there,
                send_sem=send_sems.at[0],
                recv_sem=recv_sems.at[step],
                device_id=sibling,
                device_id_type=MESH,
            ).wait_recv()
            return 0

        lax.fori_loop(0, 28, landed, 0)


def backward(xt, spread_b, point_weight, taps, runs, rows):
    width, out_count = point_weight.shape
    total_runs, total_rows, _ = spread_b.shape
    half = width // 2
    tap_index = lambda t: (jnp.maximum(t - 1, 0), 0, 0)
    return pl.pallas_call(
        functools.partial(backward_kernel, runs, rows),
        grid=(28,),
        out_shape=(
            jax.ShapeDtypeStruct((runs * rows, width), jnp.bfloat16),
            jax.ShapeDtypeStruct((28, width, out_count), jnp.bfloat16),
        ),
        in_specs=[
            pl.BlockSpec(memory_space=VMEM),
            pl.BlockSpec((total_runs, total_rows, out_count), lambda t: (0, 0, (t + 8) // 9)),
            pl.BlockSpec(memory_space=VMEM),
            pl.BlockSpec((1, width, out_count), tap_index),
        ],
        out_specs=(
            pl.BlockSpec((runs * rows, width), lambda t: (0, 0)),
            pl.BlockSpec(memory_space=pl.ANY),
        ),
        scratch_shapes=[
            VMEM((runs * rows, width), jnp.float32),
            VMEM((half, out_count), jnp.float32),
            VMEM((2, half, out_count), jnp.bfloat16),
            pltpu.SemaphoreType.DMA((2,)),
            pltpu.SemaphoreType.DMA((2,)),
            pltpu.SemaphoreType.DMA((28,)),
        ],
        compiler_params=pltpu.CompilerParams(
            dimension_semantics=("arbitrary",),
            vmem_limit_bytes=LIMIT,
            collective_id=3,
            has_side_effects=True,
        ),
        name="backward_taps",
    )(xt, spread_b, point_weight, taps)


def per_device(
    features,
    dilated_weight,
    point_weight,
    branch_gain,
    branch_shift,
    project_weight,
    project_shift,
    cotangent,
):
    local_in, tile_h, tile_w = features.shape
    out_count = point_weight.shape[1]
    local_out = branch_gain.shape[0]
    n_chan = lax.axis_size("chan")
    me = lax.axis_index("chan")
    runs, rows = tile_w // RATE_STEP, tile_h * SLOT
    used = runs * rows
    size = (-(-used // n_chan) + 15) // 16 * 16
    padded = size * n_chan
    taps = dilated_weight.reshape(27, local_in, out_count)

    vectors = jnp.concatenate([branch_gain, branch_shift, project_shift[:, None]], axis=1)
    cot = to_runs(cotangent).reshape(used, local_out)
    cot = jnp.pad(cot, ((0, padded - used), (0, 0)))
    spread_x, vectors, pw, cot = spread(
        to_runs(features), [vectors, project_weight.transpose(1, 0, 2), cot], None, 0
    )
    vectors = vectors.transpose(2, 0, 1).reshape(9, out_count)
    gain, shift, pshift = vectors[:4], vectors[4:8], vectors[8:9]
    pw = pw.transpose(1, 0, 2, 3).reshape(4, out_count, out_count)
    cot = lax.dynamic_slice_in_dim(cot, me * size, size, axis=1)
    cot = cot.transpose(1, 0, 2).reshape(size, out_count)

    part = forward(spread_x, point_weight, taps, runs, rows, size)
    mixed_out, project, grads = middle(part, gain, shift, pw, pshift, cot)
    spread_b, mixed_out, project = spread(
        grads[:used].reshape(runs, rows, 4 * out_count), [mixed_out], project, 1
    )

    total_runs, total_rows, _ = spread_x.shape
    inner = spread_x[MARGIN_RUNS:-MARGIN_RUNS, MARGIN_ROWS:-MARGIN_ROWS]
    pairs = inner.shape[0] // 2
    half = local_in // 2
    inner = lax.dynamic_slice_in_dim(inner, lax.axis_index("row") % 2 * half, half, axis=2)
    xt = inner.reshape(pairs, 2 * inner.shape[1], half).transpose(0, 2, 1)
    input_grad, weight_grads = backward(
        xt, spread_b, point_weight, taps, runs, rows
    )

    mixed_out = lax.dynamic_slice_in_dim(mixed_out, me * local_out, local_out, axis=2)
    mixed_out = from_runs(mixed_out.reshape(padded, local_out)[:used], tile_h, tile_w)
    return (
        mixed_out,
        from_runs(input_grad, tile_h, tile_w),
        weight_grads[1:].reshape(dilated_weight.shape),
        weight_grads[0],
        project.transpose(1, 0, 2),
    )


def solution(mesh):
    placed = (
        P("chan", "row", "col"),
        P(None, None, None, "chan", None),
        P("chan", None),
        P("chan", None),
        P("chan", None),
        P("chan", None, None),
        P("chan"),
        P("chan", "row", "col"),
    )
    return jax.shard_map(
        per_device,
        mesh=mesh,
        in_specs=placed,
        out_specs=(
            P("chan", "row", "col"),
            P("chan", "row", "col"),
            P(None, None, None, "chan", None),
            P("chan", None),
            P("chan", None, None),
        ),
        check_vma=False,
    )
```
